32 devices in a mesh: groups: 2 (over x), region: 16 (over z, y, core).
Axes of the slice: x: 2, y: 2, z: 4, core: 2. Of those that a mesh axis runs over, the one named last changes fastest.
Arguments:
- record: bfloat16 [16384, 640], P(('groups', 'region')), parts along dimension 0, may hold values from -6 to 6
- target: bfloat16 [4, 16384, 8192], P(None, ('groups', 'region')), parts along dimension 1, may hold values from -0.59765625 to 0.59765625
- offset: int32 [2], P('groups'), parts along dimension 0, may hold values from 0 to 127
- lag_steps: int32 [6], P('groups'), parts along dimension 0, may hold values from 1 to 8
Outputs:
- grad: float32 [16384, 640], P(('groups', 'region')), parts along dimension 0
The draws below stay inside these ranges and needn't reach their ends.
There are 2 independent parts, one for each index of `groups`. The reference program is written for one: setup_inputs(seed, part) draws one part's arguments, and reference() takes and returns one part's arrays. A program takes and returns all parts, laid end to end along the dimension named above; each array names one. Nothing has to cross between parts.
All inputs are finite; a program needn't handle non-finite values.
Results may differ from the reference program's by a relative error of at most 0.0005.
Values may be sent and summed in bfloat16 or wider, within the bound.
A program may use at most 256 MiB of HBM per device.

```python
import jax
import jax.numpy as jnp
from jax import lax

REGIONS = 8192
SAMPLES = 384
SLACK = 128
LAGS = 3
MAXLAG = 8
RECORD = 640


def level_of(rng, shape, pieces, smallest, largest):
    loudness = 1.0
    for axis_at, blocks in pieces:
        draws = jax.random.uniform(jax.random.fold_in(jax.random.fold_in(rng, 6), axis_at), (blocks,), jnp.float32, smallest / len(pieces), largest / len(pieces))
        loudness = loudness * jnp.repeat(jnp.exp(draws), shape[axis_at] // blocks).reshape((-1,) + (1,) * (len(shape) - 1 - axis_at))
    return loudness


def centred(own_key, shape, deviation, reach, pieces=(), dtype=jnp.bfloat16):
    array = deviation * jax.random.normal(own_key, shape, jnp.float32)
    if pieces:
        array = array * level_of(own_key, shape, pieces, -0.22, 0.18)
    return jnp.clip(array, -reach, reach).astype(dtype)


def setup_inputs(seed: int = 0, part: int = 0) -> dict:
    streams_of = jax.random.split(jax.random.key(seed), 5)
    part_keys = jax.random.split(jax.random.fold_in(streams_of[4], part), 5)
    return {
        "record": centred(part_keys[0], (REGIONS, RECORD), 1.0, 6.0, ((0, 16),)),
        "target": centred(part_keys[1], (1 + LAGS, REGIONS, REGIONS), 0.1, 0.59765625, ((1, 16),)),
        "offset": jax.random.randint(part_keys[2], (1,), 0, SLACK).astype(jnp.int32),
        "lag_steps": jax.random.randint(part_keys[3], (LAGS,), 1, MAXLAG + 1).astype(jnp.int32),
    }


def reference(record, target, offset, lag_steps):
    begin_at = offset[0].astype(jnp.int32)
    zero_index = jnp.zeros((), jnp.int32)
    early_view = lax.dynamic_slice_in_dim(record, begin_at, SAMPLES, 1)
    inverse = 1.0 / SAMPLES
    weight = SAMPLES / REGIONS
    cov_zero = jnp.dot(early_view, early_view.T, preferred_element_type=jnp.float32) * inverse
    target_zero = target[0].astype(jnp.float32)
    sym_err = (weight * (2.0 * cov_zero - target_zero - target_zero.T)).astype(jnp.bfloat16)
    grad_early = jnp.dot(sym_err, early_view, preferred_element_type=jnp.float32)
    blank = jnp.zeros((REGIONS, RECORD), jnp.float32)
    grad = jnp.zeros((REGIONS, RECORD), jnp.float32)
    for lag_number in range(LAGS):
        lag_value = lag_steps[lag_number].astype(jnp.int32)
        later_view = lax.dynamic_slice_in_dim(record, begin_at + lag_value, SAMPLES, 1)
        cov_lag = jnp.dot(early_view, later_view.T, preferred_element_type=jnp.float32) * inverse
        lag_err = (weight * (cov_lag - target[1 + lag_number].astype(jnp.float32))).astype(jnp.bfloat16)
        grad_early = grad_early + jnp.dot(lag_err, later_view, preferred_element_type=jnp.float32)
        grad_later = jnp.dot(lag_err.T, early_view, preferred_element_type=jnp.float32)
        grad = grad + lax.dynamic_update_slice(blank, grad_later, (zero_index, begin_at + lag_value))
    grad = grad + lax.dynamic_update_slice(blank, grad_early, (zero_index, begin_at))
    return grad
```

```python
import jax
import jax.numpy as jnp
from jax import lax
from jax.experimental import pallas as pl
from jax.experimental.pallas import tpu as pltpu
from jax.sharding import PartitionSpec as P

SAMPLES = 384
MAXLAG = 8
LAGS = 3
TERMS = 1 + LAGS
WIDE = 400
SPAN = SAMPLES + MAXLAG
WIDTH = 512
PART_A = 240


def placed_early(early, lag_steps):
    rows = early.shape[0]
    shifts = jnp.concatenate([jnp.zeros((1,), jnp.int32), lag_steps])
    padded = jnp.pad(early, ((0, 0), (MAXLAG, WIDE - SAMPLES)))
    parts = [
        lax.dynamic_slice(padded, (0, MAXLAG - shifts[term]), (rows, WIDE)) for term in range(TERMS)
    ]
    return jnp.stack(parts), shifts


def block_kernel(weight, scaled_ref, flat_ref, window_ref, target_ref, partial_ref, own_ref):
    rows = target_ref.shape[1]

    @pl.when(pl.program_id(0) == 0)
    def _():
        own_ref[...] = jnp.zeros_like(own_ref)

    window = window_ref[0]
    total = None
    for term in range(TERMS):
        cov = jnp.dot(scaled_ref[term], window, preferred_element_type=jnp.float32)
        error = (cov - weight * target_ref[term].astype(jnp.float32)).astype(jnp.bfloat16)
        own_ref[term] += lax.dot_general(
            window, error, (((1,), (1,)), ((), ())), preferred_element_type=jnp.float32
        )
        part = jnp.dot(
            flat_ref[:, term * rows : (term + 1) * rows], error, preferred_element_type=jnp.float32
        )
        total = part if total is None else total + part
    partial_ref[0] = total


def nearness(z, rank):
    low = jnp.minimum(z, 3 - z)
    seen = jnp.where((low == 1) & (rank < 2), 1 - rank, rank)
    return jnp.where(z < 2, seen, 3 - seen)


def mesh_kernel(
    flat_ref,
    turned_ref,
    target_ref,
    summed_ref,
    own_ref,
    gram_ref,
    wins,
    tiles,
    parts,
    sib_in,
    sib_out,
    yin_a,
    yin_b,
    yout_a,
    yout_b,
    zin_a,
    zin_b,
    zout_a,
    zout_b,
    tile_sem,
    win_sib_send,
    win_sib_recv,
    win_az_send,
    win_az_recv,
    win_ay_send,
    win_ay_recv,
    win_by_send,
    win_by_recv,
    win_bz_send,
    win_bz_recv,
    sum_sib_send,
    sum_sib_recv,
    sum_ay_send,
    sum_ay_recv,
    sum_az_send,
    sum_az_recv,
    sum_bz_send,
    sum_bz_recv,
    sum_by_send,
    sum_by_recv,
):
    rows = turned_ref.shape[1]
    group = lax.axis_index("groups")
    region = lax.axis_index("region")
    z = lax.div(region, 4)
    y = lax.rem(lax.div(region, 2), 2)
    k = lax.rem(region, 2)
    other = 1 - y
    sibling = 4 * z + 2 * y + 1 - k
    partner = 4 * z + 2 * other + k
    ahead = (region + 4, region - 4)
    has_next = (z < 3, z > 0)
    has_prev = (z > 0, z < 3)
    sign = (1, -1)
    first = (z, 3 - z)
    part_a = pl.ds(0, PART_A)
    part_b = pl.ds(PART_A, WIDE - PART_A)

    def chip(zz, yy):
        return 2 * zz + yy

    def remote(src, dst, send, recv, device):
        return pltpu.make_async_remote_copy(
            src_ref=src,
            dst_ref=dst,
            send_sem=send,
            recv_sem=recv,
            device_id=(group, device),
            device_id_type=pl.DeviceIdType.MESH,
        )

    def win_sib(p, lane):
        ref = wins.at[p, lane]
        return remote(ref, ref, win_sib_send.at[p], win_sib_recv.at[p], sibling)

    def win_az(way, zs):
        ref = wins.at[chip(zs, y), k, part_a]
        return remote(ref, ref, win_az_send.at[way, zs], win_az_recv.at[zs], ahead[way])

    def win_ay(zs, line):
        ref = wins.at[chip(zs, line), k, part_a]
        return remote(ref, ref, win_ay_send.at[zs], win_ay_recv.at[zs], partner)

    def win_by(line):
        ref = wins.at[chip(z, line), k, part_b]
        return remote(ref, ref, win_by_send, win_by_recv, partner)

    def win_bz(way, line, zs):
        ref = wins.at[chip(zs, line), k, part_b]
        return remote(
            ref, ref, win_bz_send.at[way, line, zs], win_bz_recv.at[line, zs], ahead[way]
        )

    def sum_sib(slot, p):
        return remote(
            sib_out.at[slot], sib_in.at[p], sum_sib_send.at[slot], sum_sib_recv.at[p], sibling
        )

    def sum_ay(zd):
        return remote(yout_a.at[zd], yin_a.at[zd], sum_ay_send.at[zd], sum_ay_recv.at[zd], partner)

    def sum_az(way, zd):
        return remote(
            zout_a.at[zd],
            zin_a.at[way, zd],
            sum_az_send.at[zd],
            sum_az_recv.at[way, zd],
            ahead[way],
        )

    def sum_bz(way, line, zd):
        return remote(
            zout_b.at[line, zd],
            zin_b.at[way, line, zd],
            sum_bz_send.at[line, zd],
            sum_bz_recv.at[way, line, zd],
            ahead[way],
        )

    def sum_by():
        return remote(yout_b, yin_b, sum_by_send, sum_by_recv, partner)

    def send_order(j):
        return nearness(z, 3 - lax.div(j, 2)), jnp.where(lax.rem(j, 2) == 0, other, y)

    def tile_chip(n):
        zd, line = send_order(n)
        m = n - 8
        zs = nearness(z, lax.div(m, 2))
        turn = jnp.where(lax.rem(m, 2) == 0, y, other)
        return jnp.where(n < 8, chip(zd, line), chip(zs, turn))

    def tile_copy(n):
        column = pl.multiple_of(tile_chip(n) * 2 * rows, 2 * rows)
        slot = lax.rem(n, 2)
        return pltpu.make_async_copy(
            target_ref.at[:, :, pl.ds(column, 2 * rows)], tiles.at[slot], tile_sem.at[slot]
        )

    def next_tile(n):
        @pl.when(n < 15)
        def _():
            tile_copy(n + 1).start()

        tile_copy(n).wait()

    tile_copy(0).start()
    here = chip(z, y)
    wins[here, k] = turned_ref[...]
    own_ref[...] = jnp.zeros_like(own_ref)
    gram_ref[...] = jnp.zeros_like(gram_ref)

    barrier = pltpu.get_barrier_semaphore()
    for device, there in (
        (sibling, None),
        (partner, None),
        (ahead[0], has_next[0]),
        (ahead[1], has_next[1]),
    ):

        def greet(device=device):
            pl.semaphore_signal(
                barrier, inc=1, device_id=(group, device), device_id_type=pl.DeviceIdType.MESH
            )

        if there is None:
            greet()
        else:
            pl.when(there)(greet)
    pl.semaphore_wait(barrier, 2 + (z < 3).astype(jnp.int32) + (z > 0).astype(jnp.int32))

    win_by(y).start()
    for way in range(2):

        @pl.when(has_next[way])
        def _():
            win_az(way, z).start()
            win_bz(way, y, z).start()

    win_sib(here, k).start()

    def collect(j):
        zd, line = send_order(j)
        p = chip(zd, line)
        sum_sib(lax.rem(j, 2), p).wait_recv()
        parts[p] += sib_in[p]

        @pl.when(lax.rem(j, 2) == 0)
        def _():
            yout_a[zd] = parts[p, part_a].astype(jnp.bfloat16)
            sum_ay(zd).start()

    def relay_a(s, way):
        zs = z - sign[way] * s
        zd = z + sign[way] * (4 - s)

        @pl.when(first[way] >= s)
        def _():
            win_az(way, zs).wait_recv()

            @pl.when(has_next[way])
            def _():
                win_az(way, zs).start()

            win_ay(zs, y).start()

        return zd

    def forward_a(s, way):
        zd = z + sign[way] * (4 - s)

        @pl.when(first[way] < s)
        def _():
            sum_ay(zd).wait_recv()
            p = chip(zd, y)

            @pl.when(has_prev[way])
            def _():
                sum_az(way, zd).wait_recv()
                zout_a[zd] = (
                    parts[p, part_a]
                    + yin_a[zd].astype(jnp.float32)
                    + zin_a[way, zd].astype(jnp.float32)
                ).astype(jnp.bfloat16)

            @pl.when(jnp.logical_not(has_prev[way]))
            def _():
                zout_a[zd] = (parts[p, part_a] + yin_a[zd].astype(jnp.float32)).astype(
                    jnp.bfloat16
                )

            sum_az(way, zd).start()

    def relay_b(s, way, line):
        zs = z - sign[way] * s

        @pl.when(first[way] >= s)
        def _():
            win_bz(way, line, zs).wait_recv()

            @pl.when(has_next[way])
            def _():
                win_bz(way, line, zs).start()

    def share(s, way):
        zs = z - sign[way] * s

        @pl.when(first[way] >= s)
        def _():
            win_sib(chip(zs, y), k).start()

    def forward_b(s, way, line):
        zd = z + sign[way] * (4 - s)

        @pl.when(first[way] < s)
        def _():
            p = chip(zd, line)

            @pl.when(has_prev[way])
            def _():
                sum_bz(way, line, zd).wait_recv()
                zout_b[line, zd] = (
                    parts[p, part_b] + zin_b[way, line, zd].astype(jnp.float32)
                ).astype(jnp.bfloat16)

            @pl.when(jnp.logical_not(has_prev[way]))
            def _():
                zout_b[line, zd] = parts[p, part_b].astype(jnp.bfloat16)

            sum_bz(way, line, zd).start()

    def bracket(s, piece):
        for way in range(2):
            if piece == 0:
                relay_a(s, way)
                forward_b(s, way, other)
            elif piece == 1:
                relay_b(s, way, y)
                share(s, way)
                forward_a(s, way)
            else:
                relay_b(s, way, other)
                forward_b(s, way, y)

    def send_step(j, carry):
        next_tile(j)
        slot = lax.rem(j, 2)
        zd, line = send_order(j)
        p = chip(zd, line)

        @pl.when(j > 1)
        def _():
            sum_sib(slot, p).wait_send()

        def product(lane):
            column = pl.multiple_of(lane * rows, rows)
            tile = tiles[slot, :, :, pl.ds(column, rows)].reshape(TERMS * rows, rows)
            return jnp.dot(flat_ref[...], tile, preferred_element_type=jnp.float32)

        sib_out[slot] = product(1 - k)
        sum_sib(slot, p).start()
        parts[p] = product(k)

        @pl.when(j > 0)
        def _():
            collect(j - 1)

        @pl.when(j == 2)
        def _():
            win_by(other).wait_recv()
            for way in range(2):

                @pl.when(has_next[way])
                def _():
                    win_bz(way, other, z).start()

            win_ay(z, y).start()

        for piece in range(3):

            @pl.when(j == 5 + piece)
            def _():
                bracket(1, piece)

        return carry

    lax.fori_loop(0, 8, send_step, 0)
    collect(7)

    def use(n, p):
        next_tile(n)
        slot = lax.rem(n, 2)
        win_sib(p, 1 - k).wait_recv()
        window = jnp.concatenate([wins[p, 0], wins[p, 1]], axis=1)
        for term in range(TERMS):
            own_ref[term] += lax.dot_general(
                window,
                tiles[slot, term],
                (((1,), (1,)), ((), ())),
                preferred_element_type=jnp.float32,
            )
        gram_ref[...] += lax.dot_general(
            window, window, (((1,), (1,)), ((), ())), preferred_element_type=jnp.float32
        )

    def use_round(rank):
        zs = nearness(z, rank)
        win_ay(zs, other).wait_recv()
        win_sib(chip(zs, other), k).start()

        def both(turn, carry):
            use(8 + 2 * rank + turn, chip(zs, jnp.where(turn == 0, y, other)))
            return carry

        lax.fori_loop(0, 2, both, 0)

    def round_step(rank, carry):
        @pl.when((rank > 0) & (rank < 3))
        def _():
            for piece in range(3):
                bracket(rank + 1, piece)

        use_round(rank)
        return carry

    lax.fori_loop(0, 4, round_step, 0)

    across = chip(z, other)
    for way in range(2):

        @pl.when(has_prev[way])
        def _():
            sum_bz(way, other, z).wait_recv()
            parts[across, part_b] += zin_b[way, other, z].astype(jnp.float32)

    yout_b[...] = parts[across, part_b].astype(jnp.bfloat16)
    sum_by().start()
    sum_ay(z).wait_recv()
    summed_ref[...] = parts[here]
    summed_ref[part_a] += yin_a[z].astype(jnp.float32)
    for way in range(2):

        @pl.when(has_prev[way])
        def _():
            sum_az(way, z).wait_recv()
            summed_ref[part_a] += zin_a[way, z].astype(jnp.float32)
            sum_bz(way, y, z).wait_recv()
            summed_ref[part_b] += zin_b[way, y, z].astype(jnp.float32)

    sum_by().wait_recv()
    summed_ref[part_b] += yin_b[...].astype(jnp.float32)

    win_by(y).wait_send()
    sum_by().wait_send()
    for slot in range(2):
        sum_sib(slot, here).wait_send()

    def drain(i, carry):
        win_ay(i, y).wait_send()
        sum_ay(i).wait_send()
        for line in range(2):
            win_sib(chip(i, line), k).wait_send()
        for way in range(2):
            reached = (i <= z, i >= z)[way]
            beyond = (i > z, i < z)[way]

            @pl.when(reached & has_next[way])
            def _():
                win_az(way, i).wait_send()
                for line in range(2):
                    win_bz(way, line, i).wait_send()

            @pl.when(beyond)
            def _():
                sum_az(way, i).wait_send()
                for line in range(2):
                    sum_bz(way, line, i).wait_send()

        return carry

    lax.fori_loop(0, 4, drain, 0)


def mesh_call(regions, flat, turned, target):
    rows = target.shape[1]
    rest = WIDE - PART_A
    work = 4 * TERMS * rows * regions * WIDE
    dma = pltpu.SemaphoreType.DMA
    half, full = jnp.bfloat16, jnp.float32
    return pl.pallas_call(
        mesh_kernel,
        in_specs=[pl.BlockSpec(memory_space=pltpu.VMEM)] * 2
        + [pl.BlockSpec(memory_space=pl.ANY)],
        out_specs=[pl.BlockSpec(memory_space=pltpu.VMEM)] * 3,
        out_shape=[
            jax.ShapeDtypeStruct((WIDE, rows), full),
            jax.ShapeDtypeStruct((TERMS, WIDE, rows), full),
            jax.ShapeDtypeStruct((WIDE, WIDE), full),
        ],
        scratch_shapes=[
            pltpu.VMEM((8, 2, WIDE, rows), half),
            pltpu.VMEM((2, TERMS, rows, 2 * rows), half),
            pltpu.VMEM((8, WIDE, rows), full),
            pltpu.VMEM((8, WIDE, rows), full),
            pltpu.VMEM((2, WIDE, rows), full),
            pltpu.VMEM((4, PART_A, rows), half),
            pltpu.VMEM((rest, rows), half),
            pltpu.VMEM((4, PART_A, rows), half),
            pltpu.VMEM((rest, rows), half),
            pltpu.VMEM((2, 4, PART_A, rows), half),
            pltpu.VMEM((2, 2, 4, rest, rows), half),
            pltpu.VMEM((4, PART_A, rows), half),
            pltpu.VMEM((2, 4, rest, rows), half),
            dma((2,)),
            dma((8,)),
            dma((8,)),
            dma((2, 4)),
            dma((4,)),
            dma((4,)),
            dma((4,)),
            dma,
            dma,
            dma((2, 2, 4)),
            dma((2, 4)),
            dma((2,)),
            dma((8,)),
            dma((4,)),
            dma((4,)),
            dma((4,)),
            dma((2, 4)),
            dma((2, 4)),
            dma((2, 2, 4)),
            dma,
            dma,
        ],
        compiler_params=pltpu.CompilerParams(
            collective_id=0, has_side_effects=True, vmem_limit_bytes=60 << 20
        ),
        cost_estimate=pl.CostEstimate(flops=work, bytes_accessed=70 << 20, transcendentals=0),
        name="mesh",
    )(flat, turned, target)


def prepare_kernel(offset_ref, lag_ref, record_ref, flat_ref, turned_ref):
    rows, length = record_ref.shape
    record = record_ref[...]
    sample = lax.broadcasted_iota(jnp.int32, (WIDE, length), 0)
    column = lax.broadcasted_iota(jnp.int32, (WIDE, length), 1) - offset_ref[0]

    def placed(pick):
        pick = jnp.where(pick, 1.0, 0.0).astype(jnp.bfloat16)
        return lax.dot_general(
            pick, record, (((1,), (1,)), ((), ())), preferred_element_type=jnp.float32
        ).astype(jnp.bfloat16)

    turned_ref[...] = placed(column == sample)
    early = (column >= 0) & (column < SAMPLES)
    for term in range(TERMS):
        lag = lag_ref[term - 1] if term else 0
        flat_ref[:, term * rows : (term + 1) * rows] = placed((column + lag == sample) & early)


def finish_kernel(
    regions, offset_ref, lag_ref, summed_ref, own_ref, gram_ref, turned_ref, grad_ref
):
    rows, length = grad_ref.shape
    gram = jnp.concatenate(
        [gram_ref[...], jnp.zeros((WIDE, WIDTH - WIDE), jnp.float32)], axis=1
    )
    inside = (lax.broadcasted_iota(jnp.int32, gram.shape, 0) < SAMPLES) & (
        lax.broadcasted_iota(jnp.int32, gram.shape, 1) < SAMPLES
    )
    early_gram = jnp.where(inside, gram, 0.0)
    before = 2.0 * gram
    after = jnp.zeros_like(gram)
    early = own_ref[0, :SAMPLES]
    for term in range(1, TERMS):
        lag = lag_ref[term - 1]
        before += pltpu.roll(pltpu.roll(gram, WIDE - lag, 0), WIDTH - lag, 1)
        after += pltpu.roll(pltpu.roll(early_gram, lag, 0), lag, 1)
        moved = own_ref[term, 1:SPAN]
        for step in (4, 2, 1):
            size = moved.shape[0] - step
            moved = jnp.where(((lag - 1) & step) > 0, moved[step:], moved[:size])
        early = early + moved
    mixed = (jnp.where(inside, before, 0.0) + after)[:, :WIDE]
    coarse = mixed.astype(jnp.bfloat16)
    fine = (mixed - coarse.astype(jnp.float32)).astype(jnp.bfloat16)
    window = turned_ref[...]
    smooth = jnp.dot(coarse, window, preferred_element_type=jnp.float32) + jnp.dot(
        fine, window, preferred_element_type=jnp.float32
    )
    weight = SAMPLES / regions
    total = smooth * (1.0 / regions) - weight * summed_ref[...]
    total = total - jnp.concatenate(
        [weight * early, jnp.zeros((WIDE - SAMPLES, rows), jnp.float32)], axis=0
    )
    sample = lax.broadcasted_iota(jnp.int32, (WIDE, length), 0)
    column = lax.broadcasted_iota(jnp.int32, (WIDE, length), 1) - offset_ref[0]
    pick = jnp.where((column == sample) & (sample < SPAN), 1.0, 0.0).astype(jnp.bfloat16)
    grad = None
    for level in range(3):
        piece = total.astype(jnp.bfloat16)
        total = total - piece.astype(jnp.float32)
        part = lax.dot_general(
            piece, pick, (((0,), (0,)), ((), ())), preferred_element_type=jnp.float32
        )
        grad = part if grad is None else grad + part
    grad_ref[...] = grad


def mesh_shards(record, target, offset, lag_steps):
    rows, length = record.shape
    regions = target.shape[2]
    vmem = pl.BlockSpec(memory_space=pltpu.VMEM)
    smem = pl.BlockSpec(memory_space=pltpu.SMEM)
    flat, turned = pl.pallas_call(
        prepare_kernel,
        in_specs=[smem, smem, vmem],
        out_specs=[vmem] * 2,
        out_shape=[
            jax.ShapeDtypeStruct((WIDE, TERMS * rows), jnp.bfloat16),
            jax.ShapeDtypeStruct((WIDE, rows), jnp.bfloat16),
        ],
        compiler_params=pltpu.CompilerParams(vmem_limit_bytes=60 << 20),
        name="prepare",
    )(offset, lag_steps, record)
    summed, own, gram = mesh_call(regions, flat, turned, target)
    return pl.pallas_call(
        lambda *refs: finish_kernel(regions, *refs),
        in_specs=[smem, smem, vmem, vmem, vmem, vmem],
        out_specs=vmem,
        out_shape=jax.ShapeDtypeStruct((rows, length), jnp.float32),
        compiler_params=pltpu.CompilerParams(vmem_limit_bytes=60 << 20),
        name="finish",
    )(offset, lag_steps, summed, own, gram, turned)


def gather_call(regions, devices, scaled, flat, turned, target):
    rows = target.shape[1]
    gathered = lax.all_gather(turned, "region")
    blocks = regions // WIDTH
    if rows != WIDTH:
        gathered = (
            gathered.reshape(blocks, WIDTH // rows, WIDE, rows)
            .transpose(0, 2, 1, 3)
            .reshape(blocks, WIDE, WIDTH)
        )
    partials, own = pl.pallas_call(
        lambda *refs: block_kernel(SAMPLES / regions, *refs),
        grid=(blocks,),
        in_specs=[
            pl.BlockSpec((TERMS, rows, WIDE), lambda i: (0, 0, 0)),
            pl.BlockSpec((SPAN, TERMS * rows), lambda i: (0, 0)),
            pl.BlockSpec((1, WIDE, WIDTH), lambda i: (i, 0, 0)),
            pl.BlockSpec((TERMS, rows, WIDTH), lambda i: (0, 0, i)),
        ],
        out_specs=[
            pl.BlockSpec((1, SPAN, WIDTH), lambda i: (i, 0, 0)),
            pl.BlockSpec((TERMS, WIDE, rows), lambda i: (0, 0, 0)),
        ],
        out_shape=[
            jax.ShapeDtypeStruct((blocks, SPAN, WIDTH), jnp.float32),
            jax.ShapeDtypeStruct((TERMS, WIDE, rows), jnp.float32),
        ],
        compiler_params=pltpu.CompilerParams(vmem_limit_bytes=56 << 20),
        name="blocks",
    )(scaled, flat, gathered, target)
    if rows != WIDTH:
        partials = (
            partials.reshape(blocks, SPAN, WIDTH // rows, rows)
            .transpose(0, 2, 1, 3)
            .reshape(devices, SPAN, rows)
        )
    summed = lax.psum_scatter(partials, "region", scatter_dimension=0, tiled=True)[0]
    return summed, own


def shards(record, target, offset, lag_steps):
    rows = record.shape[0]
    regions = target.shape[2]
    devices = lax.axis_size("region")
    if rows == WIDTH and devices == 16:
        return mesh_shards(record, target, offset, lag_steps)
    begin_at = offset[0]
    window = lax.dynamic_slice_in_dim(record, begin_at, WIDE, 1)
    stacked, shifts = placed_early(window[:, :SAMPLES], lag_steps)
    scaled = stacked * jnp.bfloat16(1.0 / regions)
    flat = stacked[:, :, :SPAN].transpose(2, 0, 1).reshape(SPAN, TERMS * rows)
    turned = window.T
    summed, own = gather_call(regions, devices, scaled, flat, turned, target)
    early = None
    for term in range(TERMS):
        part = lax.dynamic_slice(own[term], (shifts[term], 0), (SAMPLES, rows))
        early = part if early is None else early + part
    in_window = summed + jnp.pad(early, ((0, MAXLAG), (0, 0)))
    grad = jnp.zeros((record.shape[1], rows), jnp.float32)
    return lax.dynamic_update_slice(grad, in_window, (begin_at, 0)).T


def solution(mesh):
    placed = (
        P(("groups", "region"), None),
        P(None, ("groups", "region"), None),
        P("groups"),
        P("groups"),
    )
    return jax.shard_map(
        shards, mesh=mesh, in_specs=placed, out_specs=P(("groups", "region"), None), check_vma=False
    )
```

```python
import jax
import jax.numpy as jnp
from jax import lax
from jax.experimental import pallas as pl
from jax.experimental.pallas import tpu as pltpu
from jax.sharding import PartitionSpec as P

SAMPLES = 384
MAXLAG = 8
LAGS = 3
TERMS = 1 + LAGS
WIDE = 400
SPAN = SAMPLES + MAXLAG
WIDTH = 512
PART_A = 224


def placed_early(early, lag_steps):
    rows = early.shape[0]
    shifts = jnp.concatenate([jnp.zeros((1,), jnp.int32), lag_steps])
    padded = jnp.pad(early, ((0, 0), (MAXLAG, WIDE - SAMPLES)))
    parts = [
        lax.dynamic_slice(padded, (0, MAXLAG - shifts[term]), (rows, WIDE)) for term in range(TERMS)
    ]
    return jnp.stack(parts), shifts


def block_kernel(weight, scaled_ref, flat_ref, window_ref, target_ref, partial_ref, own_ref):
    rows = target_ref.shape[1]

    @pl.when(pl.program_id(0) == 0)
    def _():
        own_ref[...] = jnp.zeros_like(own_ref)

    window = window_ref[0]
    total = None
    for term in range(TERMS):
        cov = jnp.dot(scaled_ref[term], window, preferred_element_type=jnp.float32)
        error = (cov - weight * target_ref[term].astype(jnp.float32)).astype(jnp.bfloat16)
        own_ref[term] += lax.dot_general(
            window, error, (((1,), (1,)), ((), ())), preferred_element_type=jnp.float32
        )
        part = jnp.dot(
            flat_ref[:, term * rows : (term + 1) * rows], error, preferred_element_type=jnp.float32
        )
        total = part if total is None else total + part
    partial_ref[0] = total


def nearness(z, rank):
    low = jnp.minimum(z, 3 - z)
    seen = jnp.where((low == 1) & (rank < 2), 1 - rank, rank)
    return jnp.where(z < 2, seen, 3 - seen)


def mesh_kernel(
    offset_ref,
    lag_ref,
    record_ref,
    target_ref,
    grad_ref,
    flat_ref,
    own_ref,
    gram_ref,
    gram_in,
    base_ref,
    wins,
    tiles,
    parts,
    sib_in,
    sib_out,
    yin_a,
    yin_b,
    yout_a,
    yout_b,
    zin_a,
    zin_b,
    zout_a,
    zout_b,
    tile_sem,
    win_sib_send,
    win_sib_recv,
    win_az_send,
    win_az_recv,
    win_ay_send,
    win_ay_recv,
    win_by_send,
    win_by_recv,
    win_bz_send,
    win_bz_recv,
    sum_sib_send,
    sum_sib_recv,
    sum_ay_send,
    sum_ay_recv,
    sum_az_send,
    sum_az_recv,
    sum_bz_send,
    sum_bz_recv,
    sum_by_send,
    sum_by_recv,
    gram_send,
    gram_recv,
):
    rows, length = record_ref.shape
    regions = target_ref.shape[2]
    weight = SAMPLES / regions
    group = lax.axis_index("groups")
    region = lax.axis_index("region")
    z = lax.div(region, 4)
    y = lax.rem(lax.div(region, 2), 2)
    k = lax.rem(region, 2)
    other = 1 - y
    sibling = 4 * z + 2 * y + 1 - k
    partner = 4 * z + 2 * other + k
    ahead = (region + 4, region - 4)
    has_next = (z < 3, z > 0)
    has_prev = (z > 0, z < 3)
    sign = (1, -1)
    first = (z, 3 - z)
    part_a = pl.ds(0, PART_A)
    part_b = pl.ds(PART_A, WIDE - PART_A)

    def chip(zz, yy):
        return 2 * zz + yy

    def remote(src, dst, send, recv, device):
        return pltpu.make_async_remote_copy(
            src_ref=src,
            dst_ref=dst,
            send_sem=send,
            recv_sem=recv,
            device_id=(group, device),
            device_id_type=pl.DeviceIdType.MESH,
        )

    def win_sib(p, lane):
        ref = wins.at[p, lane]
        return remote(ref, ref, win_sib_send.at[p], win_sib_recv.at[p], sibling)

    def win_az(way, zs):
        ref = wins.at[chip(zs, y), k, part_a]
        return remote(ref, ref, win_az_send.at[way, zs], win_az_recv.at[zs], ahead[way])

    def win_ay(zs, line):
        ref = wins.at[chip(zs, line), k, part_a]
        return remote(ref, ref, win_ay_send.at[zs], win_ay_recv.at[zs], partner)

    def win_by(line):
        ref = wins.at[chip(z, line), k, part_b]
        return remote(ref, ref, win_by_send, win_by_recv, partner)

    def win_bz(way, line, zs):
        ref = wins.at[chip(zs, line), k, part_b]
        return remote(
            ref, ref, win_bz_send.at[way, line, zs], win_bz_recv.at[line, zs], ahead[way]
        )

    def sum_sib(slot, p):
        return remote(
            sib_out.at[slot], sib_in.at[p], sum_sib_send.at[slot], sum_sib_recv.at[p], sibling
        )

    def sum_ay(zd):
        return remote(yout_a.at[zd], yin_a.at[zd], sum_ay_send.at[zd], sum_ay_recv.at[zd], partner)

    def sum_az(way, zd):
        return remote(
            zout_a.at[zd],
            zin_a.at[way, zd],
            sum_az_send.at[zd],
            sum_az_recv.at[way, zd],
            ahead[way],
        )

    def sum_bz(way, line, zd):
        return remote(
            zout_b.at[line, zd],
            zin_b.at[way, line, zd],
            sum_bz_send.at[line, zd],
            sum_bz_recv.at[way, line, zd],
            ahead[way],
        )

    def sum_by():
        return remote(yout_b, yin_b, sum_by_send, sum_by_recv, partner)

    def send_order(j):
        return nearness(z, 3 - lax.div(j, 2)), jnp.where(lax.rem(j, 2) == 0, other, y)

    def tile_chip(n):
        zd, line = send_order(n)
        m = n - 8
        zs = nearness(z, lax.div(m, 2))
        turn = jnp.where(lax.rem(m, 2) == 0, y, other)
        return jnp.where(n < 8, chip(zd, line), chip(zs, turn))

    def tile_copy(n):
        column = pl.multiple_of(tile_chip(n) * 2 * rows, 2 * rows)
        slot = lax.rem(n, 2)
        return pltpu.make_async_copy(
            target_ref.at[:, :, pl.ds(column, 2 * rows)], tiles.at[slot], tile_sem.at[slot]
        )

    def next_tile(n):
        @pl.when(n < 15)
        def _():
            tile_copy(n + 1).start()

        tile_copy(n).wait()

    tile_copy(0).start()
    here = chip(z, y)
    barrier = pltpu.get_barrier_semaphore()
    for device, there in (
        (sibling, None),
        (partner, None),
        (ahead[0], has_next[0]),
        (ahead[1], has_next[1]),
    ):

        def greet(device=device):
            pl.semaphore_signal(
                barrier, inc=1, device_id=(group, device), device_id_type=pl.DeviceIdType.MESH
            )

        if there is None:
            greet()
        else:
            pl.when(there)(greet)
    sample = lax.broadcasted_iota(jnp.int32, (WIDE, length), 0)
    column = lax.broadcasted_iota(jnp.int32, (WIDE, length), 1) - offset_ref[0]
    pick = jnp.where(column == sample, 1.0, 0.0).astype(jnp.bfloat16)
    window = lax.dot_general(
        pick, record_ref[...], (((1,), (1,)), ((), ())), preferred_element_type=jnp.float32
    ).astype(jnp.bfloat16)
    wins[here, k] = window
    pl.semaphore_wait(barrier, 2 + (z < 3).astype(jnp.int32) + (z > 0).astype(jnp.int32))

    win_by(y).start()
    for way in range(2):

        @pl.when(has_next[way])
        def _():
            win_az(way, z).start()
            win_bz(way, y, z).start()

    win_sib(here, k).start()

    own_ref[...] = jnp.zeros_like(own_ref)
    gram_ref[...] = jnp.zeros_like(gram_ref)
    flat_ref[:SAMPLES, :rows] = window[:SAMPLES]
    flat_ref[SAMPLES:, :rows] = jnp.zeros((WIDE - SAMPLES, rows), jnp.bfloat16)
    sample = lax.broadcasted_iota(jnp.int32, (WIDE, SAMPLES), 0)
    column = lax.broadcasted_iota(jnp.int32, (WIDE, SAMPLES), 1)
    pick = jnp.concatenate(
        [jnp.where(column + lag_ref[term] == sample, 1.0, 0.0) for term in range(LAGS)]
    ).astype(jnp.bfloat16)
    moved = jnp.dot(pick, window[:SAMPLES], preferred_element_type=jnp.float32)
    for term in range(LAGS):
        flat_ref[:, (1 + term) * rows : (2 + term) * rows] = moved[
            term * WIDE : (term + 1) * WIDE
        ].astype(jnp.bfloat16)

    def collect(j):
        zd, line = send_order(j)
        p = chip(zd, line)
        sum_sib(lax.rem(j, 2), p).wait_recv()
        parts[p] += sib_in[p]

        @pl.when(lax.rem(j, 2) == 0)
        def _():
            yout_a[zd] = parts[p, part_a].astype(jnp.bfloat16)
            sum_ay(zd).start()

    def relay_a(s, way):
        zs = z - sign[way] * s
        zd = z + sign[way] * (4 - s)

        @pl.when(first[way] >= s)
        def _():
            win_az(way, zs).wait_recv()

            @pl.when(has_next[way])
            def _():
                win_az(way, zs).start()

            win_ay(zs, y).start()

        return zd

    def forward_a(s, way):
        zd = z + sign[way] * (4 - s)

        @pl.when(first[way] < s)
        def _():
            sum_ay(zd).wait_recv()
            p = chip(zd, y)

            @pl.when(has_prev[way])
            def _():
                sum_az(way, zd).wait_recv()
                zout_a[zd] = (
                    parts[p, part_a]
                    + yin_a[zd].astype(jnp.float32)
                    + zin_a[way, zd].astype(jnp.float32)
                ).astype(jnp.bfloat16)

            @pl.when(jnp.logical_not(has_prev[way]))
            def _():
                zout_a[zd] = (parts[p, part_a] + yin_a[zd].astype(jnp.float32)).astype(
                    jnp.bfloat16
                )

            sum_az(way, zd).start()

    def relay_b(s, way, line):
        zs = z - sign[way] * s

        @pl.when(first[way] >= s)
        def _():
            win_bz(way, line, zs).wait_recv()

            @pl.when(has_next[way])
            def _():
                win_bz(way, line, zs).start()

    def share(s, way):
        zs = z - sign[way] * s

        @pl.when(first[way] >= s)
        def _():
            win_sib(chip(zs, y), k).start()

    def forward_b(s, way, line):
        zd = z + sign[way] * (4 - s)

        @pl.when(first[way] < s)
        def _():
            p = chip(zd, line)

            @pl.when(has_prev[way])
            def _():
                sum_bz(way, line, zd).wait_recv()
                zout_b[line, zd] = (
                    parts[p, part_b] + zin_b[way, line, zd].astype(jnp.float32)
                ).astype(jnp.bfloat16)

            @pl.when(jnp.logical_not(has_prev[way]))
            def _():
                zout_b[line, zd] = parts[p, part_b].astype(jnp.bfloat16)

            sum_bz(way, line, zd).start()

    def bracket(s, piece):
        for way in range(2):
            if piece == 0:
                relay_a(s, way)
                forward_b(s, way, other)
            elif piece == 1:
                relay_b(s, way, y)
                share(s, way)
                forward_a(s, way)
            else:
                relay_b(s, way, other)
                forward_b(s, way, y)

    def send_step(j, carry):
        next_tile(j)
        slot = lax.rem(j, 2)
        zd, line = send_order(j)
        p = chip(zd, line)

        @pl.when(j > 1)
        def _():
            sum_sib(slot, p).wait_send()

        def product(lane):
            column = pl.multiple_of(lane * rows, rows)
            tile = tiles[slot, :, :, pl.ds(column, rows)].reshape(TERMS * rows, rows)
            return jnp.dot(flat_ref[...], tile, preferred_element_type=jnp.float32)

        sib_out[slot] = product(1 - k)
        sum_sib(slot, p).start()
        parts[p] = product(k)

        @pl.when(j > 0)
        def _():
            collect(j - 1)

        @pl.when(j == 1)
        def _():
            win_ay(z, y).start()
            win_by(other).wait_recv()
            for way in range(2):

                @pl.when(has_next[way])
                def _():
                    win_bz(way, other, z).start()

        for piece in range(3):

            @pl.when(j == 3 + piece)
            def _():
                bracket(1, piece)

        return carry

    lax.fori_loop(0, 8, send_step, 0)
    collect(7)

    def use(n, p):
        next_tile(n)
        slot = lax.rem(n, 2)
        win_sib(p, 1 - k).wait_recv()
        window = jnp.concatenate([wins[p, 0], wins[p, 1]], axis=1)
        for term in range(TERMS):
            own_ref[term] += lax.dot_general(
                window,
                tiles[slot, term],
                (((1,), (1,)), ((), ())),
                preferred_element_type=jnp.float32,
            )

    def gram_copy():
        return remote(gram_ref, gram_in, gram_send, gram_recv, sibling)

    def use_round(rank):
        zs = nearness(z, rank)
        win_ay(zs, other).wait_recv()
        win_sib(chip(zs, other), k).start()
        pair = jnp.concatenate([wins[chip(zs, y), k], wins[chip(zs, other), k]], axis=1)
        gram_ref[...] += lax.dot_general(
            pair, pair, (((1,), (1,)), ((), ())), preferred_element_type=jnp.float32
        )

        @pl.when(rank == 3)
        def _():
            gram_copy().start()

        def both(turn, carry):
            use(8 + 2 * rank + turn, chip(zs, jnp.where(turn == 0, y, other)))
            return carry

        lax.fori_loop(0, 2, both, 0)

    def round_step(rank, carry):
        @pl.when((rank > 0) & (rank < 3))
        def _():
            for piece in range(3):
                bracket(rank + 1, piece)

        use_round(rank)
        return carry

    lax.fori_loop(0, 4, round_step, 0)

    gram_copy().wait_recv()
    gram = jnp.concatenate(
        [gram_ref[...] + gram_in[...], jnp.zeros((WIDE, WIDTH - WIDE), jnp.float32)], axis=1
    )
    inside = (lax.broadcasted_iota(jnp.int32, gram.shape, 0) < SAMPLES) & (
        lax.broadcasted_iota(jnp.int32, gram.shape, 1) < SAMPLES
    )
    early_gram = jnp.where(inside, gram, 0.0)
    before = 2.0 * gram
    after = jnp.zeros_like(gram)
    early = own_ref[0, :SAMPLES]
    for term in range(LAGS):
        lag = lag_ref[term]
        before += pltpu.roll(pltpu.roll(gram, WIDE - lag, 0), WIDTH - lag, 1)
        after += pltpu.roll(pltpu.roll(early_gram, lag, 0), lag, 1)
        moved = own_ref[1 + term, 1:SPAN]
        for step in (4, 2, 1):
            size = moved.shape[0] - step
            moved = jnp.where(((lag - 1) & step) > 0, moved[step:], moved[:size])
        early = early + moved
    mixed = (jnp.where(inside, before, 0.0) + after)[:, :WIDE]
    coarse = mixed.astype(jnp.bfloat16)
    fine = (mixed - coarse.astype(jnp.float32)).astype(jnp.bfloat16)
    window = wins[here, k]
    smooth = jnp.dot(coarse, window, preferred_element_type=jnp.float32) + jnp.dot(
        fine, window, preferred_element_type=jnp.float32
    )
    base_ref[...] = smooth * (1.0 / regions) - weight * parts[here]
    base_ref[:SAMPLES] -= weight * early

    across = chip(z, other)
    for way in range(2):

        @pl.when(has_prev[way])
        def _():
            sum_bz(way, other, z).wait_recv()
            parts[across, part_b] += zin_b[way, other, z].astype(jnp.float32)

    yout_b[...] = parts[across, part_b].astype(jnp.bfloat16)
    sum_by().start()
    sum_ay(z).wait_recv()
    base_ref[part_a] -= weight * yin_a[z].astype(jnp.float32)
    for way in range(2):

        @pl.when(has_prev[way])
        def _():
            sum_az(way, z).wait_recv()
            base_ref[part_a] -= weight * zin_a[way, z].astype(jnp.float32)
            sum_bz(way, y, z).wait_recv()
            base_ref[part_b] -= weight * zin_b[way, y, z].astype(jnp.float32)

    sum_by().wait_recv()
    base_ref[part_b] -= weight * yin_b[...].astype(jnp.float32)
    result = jnp.concatenate(
        [base_ref[...].T, jnp.zeros((rows, length - WIDE), jnp.float32)], axis=1
    )
    grad_ref[...] = pltpu.roll(result, offset_ref[0], 1)

    gram_copy().wait_send()
    win_by(y).wait_send()
    sum_by().wait_send()
    for slot in range(2):
        sum_sib(slot, here).wait_send()

    def drain(i, carry):
        win_ay(i, y).wait_send()
        sum_ay(i).wait_send()
        for line in range(2):
            win_sib(chip(i, line), k).wait_send()
        for way in range(2):
            reached = (i <= z, i >= z)[way]
            beyond = (i > z, i < z)[way]

            @pl.when(reached & has_next[way])
            def _():
                win_az(way, i).wait_send()
                for line in range(2):
                    win_bz(way, line, i).wait_send()

            @pl.when(beyond)
            def _():
                sum_az(way, i).wait_send()
                for line in range(2):
                    sum_bz(way, line, i).wait_send()

        return carry

    lax.fori_loop(0, 4, drain, 0)


def mesh_shards(record, target, offset, lag_steps):
    rows, length = record.shape
    regions = target.shape[2]
    rest = WIDE - PART_A
    work = 4 * TERMS * rows * regions * WIDE
    dma = pltpu.SemaphoreType.DMA
    half, full = jnp.bfloat16, jnp.float32
    vmem = pl.BlockSpec(memory_space=pltpu.VMEM)
    smem = pl.BlockSpec(memory_space=pltpu.SMEM)
    return pl.pallas_call(
        mesh_kernel,
        in_specs=[smem, smem, vmem, pl.BlockSpec(memory_space=pl.ANY)],
        out_specs=vmem,
        out_shape=jax.ShapeDtypeStruct((rows, length), full),
        scratch_shapes=[
            pltpu.VMEM((WIDE, TERMS * rows), half),
            pltpu.VMEM((TERMS, WIDE, rows), full),
            pltpu.VMEM((WIDE, WIDE), full),
            pltpu.VMEM((WIDE, WIDE), full),
            pltpu.VMEM((WIDE, rows), full),
            pltpu.VMEM((8, 2, WIDE, rows), half),
            pltpu.VMEM((2, TERMS, rows, 2 * rows), half),
            pltpu.VMEM((8, WIDE, rows), full),
            pltpu.VMEM((8, WIDE, rows), full),
            pltpu.VMEM((2, WIDE, rows), full),
            pltpu.VMEM((4, PART_A, rows), half),
            pltpu.VMEM((rest, rows), half),
            pltpu.VMEM((4, PART_A, rows), half),
            pltpu.VMEM((rest, rows), half),
            pltpu.VMEM((2, 4, PART_A, rows), half),
            pltpu.VMEM((2, 2, 4, rest, rows), half),
            pltpu.VMEM((4, PART_A, rows), half),
            pltpu.VMEM((2, 4, rest, rows), half),
            dma((2,)),
            dma((8,)),
            dma((8,)),
            dma((2, 4)),
            dma((4,)),
            dma((4,)),
            dma((4,)),
            dma,
            dma,
            dma((2, 2, 4)),
            dma((2, 4)),
            dma((2,)),
            dma((8,)),
            dma((4,)),
            dma((4,)),
            dma((4,)),
            dma((2, 4)),
            dma((2, 4)),
            dma((2, 2, 4)),
            dma,
            dma,
            dma,
            dma,
        ],
        compiler_params=pltpu.CompilerParams(
            collective_id=0, has_side_effects=True, vmem_limit_bytes=60 << 20
        ),
        cost_estimate=pl.CostEstimate(flops=work, bytes_accessed=70 << 20, transcendentals=0),
        name="mesh",
    )(offset, lag_steps, record, target)


def gather_call(regions, devices, scaled, flat, turned, target):
    rows = target.shape[1]
    gathered = lax.all_gather(turned, "region")
    blocks = regions // WIDTH
    if rows != WIDTH:
        gathered = (
            gathered.reshape(blocks, WIDTH // rows, WIDE, rows)
            .transpose(0, 2, 1, 3)
            .reshape(blocks, WIDE, WIDTH)
        )
    partials, own = pl.pallas_call(
        lambda *refs: block_kernel(SAMPLES / regions, *refs),
        grid=(blocks,),
        in_specs=[
            pl.BlockSpec((TERMS, rows, WIDE), lambda i: (0, 0, 0)),
            pl.BlockSpec((SPAN, TERMS * rows), lambda i: (0, 0)),
            pl.BlockSpec((1, WIDE, WIDTH), lambda i: (i, 0, 0)),
            pl.BlockSpec((TERMS, rows, WIDTH), lambda i: (0, 0, i)),
        ],
        out_specs=[
            pl.BlockSpec((1, SPAN, WIDTH), lambda i: (i, 0, 0)),
            pl.BlockSpec((TERMS, WIDE, rows), lambda i: (0, 0, 0)),
        ],
        out_shape=[
            jax.ShapeDtypeStruct((blocks, SPAN, WIDTH), jnp.float32),
            jax.ShapeDtypeStruct((TERMS, WIDE, rows), jnp.float32),
        ],
        compiler_params=pltpu.CompilerParams(vmem_limit_bytes=56 << 20),
        name="blocks",
    )(scaled, flat, gathered, target)
    if rows != WIDTH:
        partials = (
            partials.reshape(blocks, SPAN, WIDTH // rows, rows)
            .transpose(0, 2, 1, 3)
            .reshape(devices, SPAN, rows)
        )
    summed = lax.psum_scatter(partials, "region", scatter_dimension=0, tiled=True)[0]
    return summed, own


def shards(record, target, offset, lag_steps):
    rows = record.shape[0]
    regions = target.shape[2]
    devices = lax.axis_size("region")
    if rows == WIDTH and devices == 16:
        return mesh_shards(record, target, offset, lag_steps)
    begin_at = offset[0]
    window = lax.dynamic_slice_in_dim(record, begin_at, WIDE, 1)
    stacked, shifts = placed_early(window[:, :SAMPLES], lag_steps)
    scaled = stacked * jnp.bfloat16(1.0 / regions)
    flat = stacked[:, :, :SPAN].transpose(2, 0, 1).reshape(SPAN, TERMS * rows)
    turned = window.T
    summed, own = gather_call(regions, devices, scaled, flat, turned, target)
    early = None
    for term in range(TERMS):
        part = lax.dynamic_slice(own[term], (shifts[term], 0), (SAMPLES, rows))
        early = part if early is None else early + part
    in_window = summed + jnp.pad(early, ((0, MAXLAG), (0, 0)))
    grad = jnp.zeros((record.shape[1], rows), jnp.float32)
    return lax.dynamic_update_slice(grad, in_window, (begin_at, 0)).T


def solution(mesh):
    placed = (
        P(("groups", "region"), None),
        P(None, ("groups", "region"), None),
        P("groups"),
        P("groups"),
    )
    return jax.shard_map(
        shards, mesh=mesh, in_specs=placed, out_specs=P(("groups", "region"), None), check_vma=False
    )
```

```python
import jax
import jax.numpy as jnp
from jax import lax
from jax.experimental import pallas as pl
from jax.experimental.pallas import tpu as pltpu
from jax.sharding import PartitionSpec as P

SAMPLES = 384
MAXLAG = 8
LAGS = 3
TERMS = 1 + LAGS
WIDE = 400
SPAN = SAMPLES + MAXLAG
WIDTH = 512
PART_A = 224


def placed_early(early, lag_steps):
    rows = early.shape[0]
    shifts = jnp.concatenate([jnp.zeros((1,), jnp.int32), lag_steps])
    padded = jnp.pad(early, ((0, 0), (MAXLAG, WIDE - SAMPLES)))
    parts = [
        lax.dynamic_slice(padded, (0, MAXLAG - shifts[term]), (rows, WIDE)) for term in range(TERMS)
    ]
    return jnp.stack(parts), shifts


def block_kernel(weight, scaled_ref, flat_ref, window_ref, target_ref, partial_ref, own_ref):
    rows = target_ref.shape[1]

    @pl.when(pl.program_id(0) == 0)
    def _():
        own_ref[...] = jnp.zeros_like(own_ref)

    window = window_ref[0]
    total = None
    for term in range(TERMS):
        cov = jnp.dot(scaled_ref[term], window, preferred_element_type=jnp.float32)
        error = (cov - weight * target_ref[term].astype(jnp.float32)).astype(jnp.bfloat16)
        own_ref[term] += lax.dot_general(
            window, error, (((1,), (1,)), ((), ())), preferred_element_type=jnp.float32
        )
        part = jnp.dot(
            flat_ref[:, term * rows : (term + 1) * rows], error, preferred_element_type=jnp.float32
        )
        total = part if total is None else total + part
    partial_ref[0] = total


def nearness(z, rank):
    low = jnp.minimum(z, 3 - z)
    seen = jnp.where((low == 1) & (rank < 2), 1 - rank, rank)
    return jnp.where(z < 2, seen, 3 - seen)


def mesh_kernel(
    offset_ref,
    lag_ref,
    record_ref,
    target_ref,
    grad_ref,
    flat_ref,
    own_ref,
    gram_ref,
    gram_in,
    base_ref,
    wins,
    tiles,
    parts,
    sib_in,
    sib_out,
    yin_a,
    yin_b,
    yout_a,
    yout_b,
    zin_a,
    zin_b,
    zout_a,
    zout_b,
    tile_sem,
    win_sib_send,
    win_sib_recv,
    win_az_send,
    win_az_recv,
    win_ay_send,
    win_ay_recv,
    win_by_send,
    win_by_recv,
    win_bz_send,
    win_bz_recv,
    sum_sib_send,
    sum_sib_recv,
    sum_ay_send,
    sum_ay_recv,
    sum_az_send,
    sum_az_recv,
    sum_bz_send,
    sum_bz_recv,
    sum_by_send,
    sum_by_recv,
    gram_send,
    gram_recv,
):
    rows, length = record_ref.shape
    regions = target_ref.shape[2]
    weight = SAMPLES / regions
    group = lax.axis_index("groups")
    region = lax.axis_index("region")
    z = lax.div(region, 4)
    y = lax.rem(lax.div(region, 2), 2)
    k = lax.rem(region, 2)
    other = 1 - y
    sibling = 4 * z + 2 * y + 1 - k
    partner = 4 * z + 2 * other + k
    ahead = (region + 4, region - 4)
    has_next = (z < 3, z > 0)
    has_prev = (z > 0, z < 3)
    sign = (1, -1)
    first = (z, 3 - z)
    part_a = pl.ds(0, PART_A)
    part_b = pl.ds(PART_A, WIDE - PART_A)

    def chip(zz, yy):
        return 2 * zz + yy

    def remote(src, dst, send, recv, device):
        return pltpu.make_async_remote_copy(
            src_ref=src,
            dst_ref=dst,
            send_sem=send,
            recv_sem=recv,
            device_id=(group, device),
            device_id_type=pl.DeviceIdType.MESH,
        )

    def win_sib(p, lane):
        ref = wins.at[p, lane]
        return remote(ref, ref, win_sib_send.at[p], win_sib_recv.at[p], sibling)

    def win_az(way, zs):
        ref = wins.at[chip(zs, y), k, part_a]
        return remote(ref, ref, win_az_send.at[way, zs], win_az_recv.at[zs], ahead[way])

    def win_ay(zs, line):
        ref = wins.at[chip(zs, line), k, part_a]
        return remote(ref, ref, win_ay_send.at[zs], win_ay_recv.at[zs], partner)

    def win_by(line):
        ref = wins.at[chip(z, line), k, part_b]
        return remote(ref, ref, win_by_send, win_by_recv, partner)

    def win_bz(way, line, zs):
        ref = wins.at[chip(zs, line), k, part_b]
        return remote(
            ref, ref, win_bz_send.at[way, line, zs], win_bz_recv.at[line, zs], ahead[way]
        )

    def sum_sib(slot, p):
        return remote(
            sib_out.at[slot], sib_in.at[p], sum_sib_send.at[slot], sum_sib_recv.at[p], sibling
        )

    def sum_ay(zd):
        return remote(yout_a.at[zd], yin_a.at[zd], sum_ay_send.at[zd], sum_ay_recv.at[zd], partner)

    def sum_az(way, zd):
        return remote(
            zout_a.at[zd],
            zin_a.at[way, zd],
            sum_az_send.at[zd],
            sum_az_recv.at[way, zd],
            ahead[way],
        )

    def sum_bz(way, line, zd):
        return remote(
            zout_b.at[line, zd],
            zin_b.at[way, line, zd],
            sum_bz_send.at[line, zd],
            sum_bz_recv.at[way, line, zd],
            ahead[way],
        )

    def sum_by():
        return remote(yout_b, yin_b, sum_by_send, sum_by_recv, partner)

    def send_order(j):
        return nearness(z, 3 - lax.div(j, 2)), jnp.where(lax.rem(j, 2) == 0, other, y)

    def tile_chip(n):
        zd, line = send_order(n)
        m = n - 8
        zs = nearness(z, lax.div(m, 2))
        turn = jnp.where(lax.rem(m, 2) == 0, y, other)
        return jnp.where(n < 8, chip(zd, line), chip(zs, turn))

    def tile_copy(n):
        column = pl.multiple_of(tile_chip(n) * 2 * rows, 2 * rows)
        slot = lax.rem(n, 2)
        return pltpu.make_async_copy(
            target_ref.at[:, :, pl.ds(column, 2 * rows)], tiles.at[slot], tile_sem.at[slot]
        )

    def next_tile(n):
        @pl.when(n < 15)
        def _():
            tile_copy(n + 1).start()

        tile_copy(n).wait()

    tile_copy(0).start()
    here = chip(z, y)
    barrier = pltpu.get_barrier_semaphore()
    for device, there in (
        (sibling, None),
        (partner, None),
        (ahead[0], has_next[0]),
        (ahead[1], has_next[1]),
    ):

        def greet(device=device):
            pl.semaphore_signal(
                barrier, inc=1, device_id=(group, device), device_id_type=pl.DeviceIdType.MESH
            )

        if there is None:
            greet()
        else:
            pl.when(there)(greet)
    sample = lax.broadcasted_iota(jnp.int32, (WIDE, length), 0)
    column = lax.broadcasted_iota(jnp.int32, (WIDE, length), 1) - offset_ref[0]
    pick = jnp.where(column == sample, 1.0, 0.0).astype(jnp.bfloat16)
    window = lax.dot_general(
        pick, record_ref[...], (((1,), (1,)), ((), ())), preferred_element_type=jnp.float32
    ).astype(jnp.bfloat16)
    wins[here, k] = window
    pl.semaphore_wait(barrier, 2 + (z < 3).astype(jnp.int32) + (z > 0).astype(jnp.int32))

    win_by(y).start()
    for way in range(2):

        @pl.when(has_next[way])
        def _():
            win_az(way, z).start()
            win_bz(way, y, z).start()

    win_sib(here, k).start()

    own_ref[...] = jnp.zeros_like(own_ref)
    gram_ref[...] = jnp.zeros_like(gram_ref)
    flat_ref[:SAMPLES, :rows] = window[:SAMPLES]
    flat_ref[SAMPLES:, :rows] = jnp.zeros((WIDE - SAMPLES, rows), jnp.bfloat16)
    sample = lax.broadcasted_iota(jnp.int32, (WIDE, SAMPLES), 0)
    column = lax.broadcasted_iota(jnp.int32, (WIDE, SAMPLES), 1)
    pick = jnp.concatenate(
        [jnp.where(column + lag_ref[term] == sample, 1.0, 0.0) for term in range(LAGS)]
    ).astype(jnp.bfloat16)
    moved = jnp.dot(pick, window[:SAMPLES], preferred_element_type=jnp.float32)
    for term in range(LAGS):
        flat_ref[:, (1 + term) * rows : (2 + term) * rows] = moved[
            term * WIDE : (term + 1) * WIDE
        ].astype(jnp.bfloat16)

    def collect(j):
        zd, line = send_order(j)
        p = chip(zd, line)
        sum_sib(lax.rem(j, 2), p).wait_recv()
        parts[p] += sib_in[p]

        @pl.when(lax.rem(j, 2) == 0)
        def _():
            yout_a[zd] = parts[p, part_a].astype(jnp.bfloat16)
            sum_ay(zd).start()

    def relay_a(s, way):
        zs = z - sign[way] * s
        zd = z + sign[way] * (4 - s)

        @pl.when(first[way] >= s)
        def _():
            win_az(way, zs).wait_recv()

            @pl.when(has_next[way])
            def _():
                win_az(way, zs).start()

            win_ay(zs, y).start()

        return zd

    def forward_a(s, way):
        zd = z + sign[way] * (4 - s)

        @pl.when(first[way] < s)
        def _():
            sum_ay(zd).wait_recv()
            p = chip(zd, y)

            @pl.when(has_prev[way])
            def _():
                sum_az(way, zd).wait_recv()
                zout_a[zd] = (
                    parts[p, part_a]
                    + yin_a[zd].astype(jnp.float32)
                    + zin_a[way, zd].astype(jnp.float32)
                ).astype(jnp.bfloat16)

            @pl.when(jnp.logical_not(has_prev[way]))
            def _():
                zout_a[zd] = (parts[p, part_a] + yin_a[zd].astype(jnp.float32)).astype(
                    jnp.bfloat16
                )

            sum_az(way, zd).start()

    def relay_b(s, way, line):
        zs = z - sign[way] * s

        @pl.when(first[way] >= s)
        def _():
            win_bz(way, line, zs).wait_recv()

            @pl.when(has_next[way])
            def _():
                win_bz(way, line, zs).start()

    def share(s, way):
        zs = z - sign[way] * s

        @pl.when(first[way] >= s)
        def _():
            win_sib(chip(zs, y), k).start()

    def forward_b(s, way, line):
        zd = z + sign[way] * (4 - s)

        @pl.when(first[way] < s)
        def _():
            p = chip(zd, line)

            @pl.when(has_prev[way])
            def _():
                sum_bz(way, line, zd).wait_recv()
                zout_b[line, zd] = (
                    parts[p, part_b] + zin_b[way, line, zd].astype(jnp.float32)
                ).astype(jnp.bfloat16)

            @pl.when(jnp.logical_not(has_prev[way]))
            def _():
                zout_b[line, zd] = parts[p, part_b].astype(jnp.bfloat16)

            sum_bz(way, line, zd).start()

    def bracket(s, piece):
        for way in range(2):
            if piece == 0:
                relay_a(s, way)
                forward_b(s, way, other)
            elif piece == 1:
                relay_b(s, way, y)
                share(s, way)
                forward_a(s, way)
            else:
                relay_b(s, way, other)
                forward_b(s, way, y)

    def pass_on():
        win_by(other).wait_recv()
        for way in range(2):

            @pl.when(has_next[way])
            def _():
                win_bz(way, other, z).start()

    def finish_across():
        across = chip(z, other)
        for way in range(2):

            @pl.when(has_prev[way])
            def _():
                sum_bz(way, other, z).wait_recv()
                parts[across, part_b] += zin_b[way, other, z].astype(jnp.float32)

        yout_b[...] = parts[across, part_b].astype(jnp.bfloat16)
        sum_by().start()

    def at(step, table):
        for when, actions in table:

            @pl.when(step == when)
            def _():
                for action in actions:
                    action()

    def relay(s, piece):
        return lambda: bracket(s, piece)

    def send_step(j, carry):
        at(
            j,
            (
                (1, (lambda: win_ay(z, y).start(),)),
                (2, (pass_on,)),
                (3, (relay(1, 0),)),
                (5, (relay(1, 1),)),
                (6, (relay(1, 2),)),
                (7, (relay(2, 0),)),
            ),
        )
        next_tile(j)
        slot = lax.rem(j, 2)
        zd, line = send_order(j)
        p = chip(zd, line)

        @pl.when(j > 1)
        def _():
            sum_sib(slot, p).wait_send()

        def product(lane):
            column = pl.multiple_of(lane * rows, rows)
            tile = tiles[slot, :, :, pl.ds(column, rows)].reshape(TERMS * rows, rows)
            return jnp.dot(flat_ref[...], tile, preferred_element_type=jnp.float32)

        sib_out[slot] = product(1 - k)
        sum_sib(slot, p).start()
        parts[p] = product(k)

        @pl.when(j > 0)
        def _():
            collect(j - 1)

        return carry

    lax.fori_loop(0, 8, send_step, 0)
    bracket(2, 1)
    bracket(2, 2)
    collect(7)

    def use(n, p):
        next_tile(n)
        slot = lax.rem(n, 2)
        win_sib(p, 1 - k).wait_recv()
        window = jnp.concatenate([wins[p, 0], wins[p, 1]], axis=1)
        for term in range(TERMS):
            own_ref[term] += lax.dot_general(
                window,
                tiles[slot, term],
                (((1,), (1,)), ((), ())),
                preferred_element_type=jnp.float32,
            )

    def gram_copy():
        return remote(gram_ref, gram_in, gram_send, gram_recv, sibling)

    def open_round(rank):
        zs = nearness(z, rank)
        win_ay(zs, other).wait_recv()
        win_sib(chip(zs, other), k).start()
        pair = jnp.concatenate([wins[chip(zs, y), k], wins[chip(zs, other), k]], axis=1)
        gram_ref[...] += lax.dot_general(
            pair, pair, (((1,), (1,)), ((), ())), preferred_element_type=jnp.float32
        )

        @pl.when(rank == 3)
        def _():
            gram_copy().start()

    def use_step(n, carry):
        at(n, ((3, (relay(3, 0),)), (5, (relay(3, 1),)), (6, (relay(3, 2), finish_across))))
        rank = lax.div(n, 2)

        @pl.when(lax.rem(n, 2) == 0)
        def _():
            open_round(rank)

        use(8 + n, chip(nearness(z, rank), jnp.where(lax.rem(n, 2) == 0, y, other)))
        return carry

    lax.fori_loop(0, 8, use_step, 0)

    gram_copy().wait_recv()
    gram = jnp.concatenate(
        [gram_ref[...] + gram_in[...], jnp.zeros((WIDE, WIDTH - WIDE), jnp.float32)], axis=1
    )
    inside = (lax.broadcasted_iota(jnp.int32, gram.shape, 0) < SAMPLES) & (
        lax.broadcasted_iota(jnp.int32, gram.shape, 1) < SAMPLES
    )
    early_gram = jnp.where(inside, gram, 0.0)
    before = 2.0 * gram
    after = jnp.zeros_like(gram)
    early = own_ref[0, :SAMPLES]
    for term in range(LAGS):
        lag = lag_ref[term]
        before += pltpu.roll(pltpu.roll(gram, WIDE - lag, 0), WIDTH - lag, 1)
        after += pltpu.roll(pltpu.roll(early_gram, lag, 0), lag, 1)
        moved = own_ref[1 + term, 1:SPAN]
        for step in (4, 2, 1):
            size = moved.shape[0] - step
            moved = jnp.where(((lag - 1) & step) > 0, moved[step:], moved[:size])
        early = early + moved
    mixed = (jnp.where(inside, before, 0.0) + after)[:, :WIDE]
    coarse = mixed.astype(jnp.bfloat16)
    fine = (mixed - coarse.astype(jnp.float32)).astype(jnp.bfloat16)
    window = wins[here, k]
    smooth = jnp.dot(coarse, window, preferred_element_type=jnp.float32) + jnp.dot(
        fine, window, preferred_element_type=jnp.float32
    )
    base_ref[...] = smooth * (1.0 / regions) - weight * parts[here]
    base_ref[:SAMPLES] -= weight * early

    sum_ay(z).wait_recv()
    base_ref[part_a] -= weight * yin_a[z].astype(jnp.float32)
    for way in range(2):

        @pl.when(has_prev[way])
        def _():
            sum_az(way, z).wait_recv()
            base_ref[part_a] -= weight * zin_a[way, z].astype(jnp.float32)
            sum_bz(way, y, z).wait_recv()
            base_ref[part_b] -= weight * zin_b[way, y, z].astype(jnp.float32)

    sum_by().wait_recv()
    base_ref[part_b] -= weight * yin_b[...].astype(jnp.float32)
    result = jnp.concatenate(
        [base_ref[...].T, jnp.zeros((rows, length - WIDE), jnp.float32)], axis=1
    )
    grad_ref[...] = pltpu.roll(result, offset_ref[0], 1)

    gram_copy().wait_send()
    win_by(y).wait_send()
    sum_by().wait_send()
    for slot in range(2):
        sum_sib(slot, here).wait_send()

    def drain(i, carry):
        win_ay(i, y).wait_send()
        sum_ay(i).wait_send()
        for line in range(2):
            win_sib(chip(i, line), k).wait_send()
        for way in range(2):
            reached = (i <= z, i >= z)[way]
            beyond = (i > z, i < z)[way]

            @pl.when(reached & has_next[way])
            def _():
                win_az(way, i).wait_send()
                for line in range(2):
                    win_bz(way, line, i).wait_send()

            @pl.when(beyond)
            def _():
                sum_az(way, i).wait_send()
                for line in range(2):
                    sum_bz(way, line, i).wait_send()

        return carry

    lax.fori_loop(0, 4, drain, 0)


def mesh_shards(record, target, offset, lag_steps):
    rows, length = record.shape
    regions = target.shape[2]
    rest = WIDE - PART_A
    work = 4 * TERMS * rows * regions * WIDE
    dma = pltpu.SemaphoreType.DMA
    half, full = jnp.bfloat16, jnp.float32
    vmem = pl.BlockSpec(memory_space=pltpu.VMEM)
    smem = pl.BlockSpec(memory_space=pltpu.SMEM)
    return pl.pallas_call(
        mesh_kernel,
        in_specs=[smem, smem, vmem, pl.BlockSpec(memory_space=pl.ANY)],
        out_specs=vmem,
        out_shape=jax.ShapeDtypeStruct((rows, length), full),
        scratch_shapes=[
            pltpu.VMEM((WIDE, TERMS * rows), half),
            pltpu.VMEM((TERMS, WIDE, rows), full),
            pltpu.VMEM((WIDE, WIDE), full),
            pltpu.VMEM((WIDE, WIDE), full),
            pltpu.VMEM((WIDE, rows), full),
            pltpu.VMEM((8, 2, WIDE, rows), half),
            pltpu.VMEM((2, TERMS, rows, 2 * rows), half),
            pltpu.VMEM((8, WIDE, rows), full),
            pltpu.VMEM((8, WIDE, rows), full),
            pltpu.VMEM((2, WIDE, rows), full),
            pltpu.VMEM((4, PART_A, rows), half),
            pltpu.VMEM((rest, rows), half),
            pltpu.VMEM((4, PART_A, rows), half),
            pltpu.VMEM((rest, rows), half),
            pltpu.VMEM((2, 4, PART_A, rows), half),
            pltpu.VMEM((2, 2, 4, rest, rows), half),
            pltpu.VMEM((4, PART_A, rows), half),
            pltpu.VMEM((2, 4, rest, rows), half),
            dma((2,)),
            dma((8,)),
            dma((8,)),
            dma((2, 4)),
            dma((4,)),
            dma((4,)),
            dma((4,)),
            dma,
            dma,
            dma((2, 2, 4)),
            dma((2, 4)),
            dma((2,)),
            dma((8,)),
            dma((4,)),
            dma((4,)),
            dma((4,)),
            dma((2, 4)),
            dma((2, 4)),
            dma((2, 2, 4)),
            dma,
            dma,
            dma,
            dma,
        ],
        compiler_params=pltpu.CompilerParams(
            collective_id=0, has_side_effects=True, vmem_limit_bytes=60 << 20
        ),
        cost_estimate=pl.CostEstimate(flops=work, bytes_accessed=70 << 20, transcendentals=0),
        name="mesh",
    )(offset, lag_steps, record, target)


def gather_call(regions, devices, scaled, flat, turned, target):
    rows = target.shape[1]
    gathered = lax.all_gather(turned, "region")
    blocks = regions // WIDTH
    if rows != WIDTH:
        gathered = (
            gathered.reshape(blocks, WIDTH // rows, WIDE, rows)
            .transpose(0, 2, 1, 3)
            .reshape(blocks, WIDE, WIDTH)
        )
    partials, own = pl.pallas_call(
        lambda *refs: block_kernel(SAMPLES / regions, *refs),
        grid=(blocks,),
        in_specs=[
            pl.BlockSpec((TERMS, rows, WIDE), lambda i: (0, 0, 0)),
            pl.BlockSpec((SPAN, TERMS * rows), lambda i: (0, 0)),
            pl.BlockSpec((1, WIDE, WIDTH), lambda i: (i, 0, 0)),
            pl.BlockSpec((TERMS, rows, WIDTH), lambda i: (0, 0, i)),
        ],
        out_specs=[
            pl.BlockSpec((1, SPAN, WIDTH), lambda i: (i, 0, 0)),
            pl.BlockSpec((TERMS, WIDE, rows), lambda i: (0, 0, 0)),
        ],
        out_shape=[
            jax.ShapeDtypeStruct((blocks, SPAN, WIDTH), jnp.float32),
            jax.ShapeDtypeStruct((TERMS, WIDE, rows), jnp.float32),
        ],
        compiler_params=pltpu.CompilerParams(vmem_limit_bytes=56 << 20),
        name="blocks",
    )(scaled, flat, gathered, target)
    if rows != WIDTH:
        partials = (
            partials.reshape(blocks, SPAN, WIDTH // rows, rows)
            .transpose(0, 2, 1, 3)
            .reshape(devices, SPAN, rows)
        )
    summed = lax.psum_scatter(partials, "region", scatter_dimension=0, tiled=True)[0]
    return summed, own


def shards(record, target, offset, lag_steps):
    rows = record.shape[0]
    regions = target.shape[2]
    devices = lax.axis_size("region")
    if rows == WIDTH and devices == 16:
        return mesh_shards(record, target, offset, lag_steps)
    begin_at = offset[0]
    window = lax.dynamic_slice_in_dim(record, begin_at, WIDE, 1)
    stacked, shifts = placed_early(window[:, :SAMPLES], lag_steps)
    scaled = stacked * jnp.bfloat16(1.0 / regions)
    flat = stacked[:, :, :SPAN].transpose(2, 0, 1).reshape(SPAN, TERMS * rows)
    turned = window.T
    summed, own = gather_call(regions, devices, scaled, flat, turned, target)
    early = None
    for term in range(TERMS):
        part = lax.dynamic_slice(own[term], (shifts[term], 0), (SAMPLES, rows))
        early = part if early is None else early + part
    in_window = summed + jnp.pad(early, ((0, MAXLAG), (0, 0)))
    grad = jnp.zeros((record.shape[1], rows), jnp.float32)
    return lax.dynamic_update_slice(grad, in_window, (begin_at, 0)).T


def solution(mesh):
    placed = (
        P(("groups", "region"), None),
        P(None, ("groups", "region"), None),
        P("groups"),
        P("groups"),
    )
    return jax.shard_map(
        shards, mesh=mesh, in_specs=placed, out_specs=P(("groups", "region"), None), check_vma=False
    )
```

```python
import jax
import jax.numpy as jnp
from jax import lax
from jax.experimental import pallas as pl
from jax.experimental.pallas import tpu as pltpu
from jax.sharding import PartitionSpec as P

SAMPLES = 384
MAXLAG = 8
LAGS = 3
TERMS = 1 + LAGS
WIDE = 400
SPAN = SAMPLES + MAXLAG
WIDTH = 512
PART_A = 240
SLAB = 128


def placed_early(early, lag_steps):
    rows = early.shape[0]
    shifts = jnp.concatenate([jnp.zeros((1,), jnp.int32), lag_steps])
    padded = jnp.pad(early, ((0, 0), (MAXLAG, WIDE - SAMPLES)))
    parts = [
        lax.dynamic_slice(padded, (0, MAXLAG - shifts[term]), (rows, WIDE)) for term in range(TERMS)
    ]
    return jnp.stack(parts), shifts


def block_kernel(weight, scaled_ref, flat_ref, window_ref, target_ref, partial_ref, own_ref):
    rows = target_ref.shape[1]

    @pl.when(pl.program_id(0) == 0)
    def _():
        own_ref[...] = jnp.zeros_like(own_ref)

    window = window_ref[0]
    total = None
    for term in range(TERMS):
        cov = jnp.dot(scaled_ref[term], window, preferred_element_type=jnp.float32)
        error = (cov - weight * target_ref[term].astype(jnp.float32)).astype(jnp.bfloat16)
        own_ref[term] += lax.dot_general(
            window, error, (((1,), (1,)), ((), ())), preferred_element_type=jnp.float32
        )
        part = jnp.dot(
            flat_ref[:, term * rows : (term + 1) * rows], error, preferred_element_type=jnp.float32
        )
        total = part if total is None else total + part
    partial_ref[0] = total


def nearness(z, rank):
    low = jnp.minimum(z, 3 - z)
    seen = jnp.where((low == 1) & (rank < 2), 1 - rank, rank)
    return jnp.where(z < 2, seen, 3 - seen)


def mesh_kernel(
    offset_ref,
    lag_ref,
    record_ref,
    target_ref,
    grad_ref,
    flat_ref,
    own_ref,
    gram_ref,
    gram_in,
    base_ref,
    held,
    result,
    wins,
    tiles,
    parts,
    sib_in,
    sib_out,
    yin_a,
    yin_b,
    yout_a,
    yout_b,
    zin_a,
    zin_b,
    zout_a,
    zout_b,
    record_sem,
    grad_sem,
    tile_sem,
    win_sib_send,
    win_sib_recv,
    win_az_send,
    win_az_recv,
    win_ay_send,
    win_ay_recv,
    win_by_send,
    win_by_recv,
    win_bz_send,
    win_bz_recv,
    sum_sib_send,
    sum_sib_recv,
    sum_ay_send,
    sum_ay_recv,
    sum_az_send,
    sum_az_recv,
    sum_bz_send,
    sum_bz_recv,
    sum_by_send,
    sum_by_recv,
    gram_send,
    gram_recv,
):
    rows, length = record_ref.shape
    regions = target_ref.shape[2]
    weight = SAMPLES / regions
    group = lax.axis_index("groups")
    region = lax.axis_index("region")
    z = lax.div(region, 4)
    y = lax.rem(lax.div(region, 2), 2)
    k = lax.rem(region, 2)
    other = 1 - y
    sibling = 4 * z + 2 * y + 1 - k
    partner = 4 * z + 2 * other + k
    ahead = (region + 4, region - 4)
    has_next = (z < 3, z > 0)
    has_prev = (z > 0, z < 3)
    sign = (1, -1)
    first = (z, 3 - z)
    part_a = pl.ds(0, PART_A)
    part_b = pl.ds(PART_A, WIDE - PART_A)

    def chip(zz, yy):
        return 2 * zz + yy

    def remote(src, dst, send, recv, device):
        return pltpu.make_async_remote_copy(
            src_ref=src,
            dst_ref=dst,
            send_sem=send,
            recv_sem=recv,
            device_id=(group, device),
            device_id_type=pl.DeviceIdType.MESH,
        )

    def win_sib(p, lane):
        ref = wins.at[p, lane]
        return remote(ref, ref, win_sib_send.at[p], win_sib_recv.at[p], sibling)

    def win_az(way, zs):
        ref = wins.at[chip(zs, y), k, part_a]
        return remote(ref, ref, win_az_send.at[way, zs], win_az_recv.at[zs], ahead[way])

    def win_ay(zs, line):
        ref = wins.at[chip(zs, line), k, part_a]
        return remote(ref, ref, win_ay_send.at[zs], win_ay_recv.at[zs], partner)

    def win_by(line):
        ref = wins.at[chip(z, line), k, part_b]
        return remote(ref, ref, win_by_send, win_by_recv, partner)

    def win_bz(way, line, zs):
        ref = wins.at[chip(zs, line), k, part_b]
        return remote(
            ref, ref, win_bz_send.at[way, line, zs], win_bz_recv.at[line, zs], ahead[way]
        )

    def sum_sib(slot, p):
        return remote(
            sib_out.at[slot], sib_in.at[p], sum_sib_send.at[slot], sum_sib_recv.at[p], sibling
        )

    def sum_ay(zd):
        return remote(yout_a.at[zd], yin_a.at[zd], sum_ay_send.at[zd], sum_ay_recv.at[zd], partner)

    def sum_az(way, zd):
        return remote(
            zout_a.at[zd],
            zin_a.at[way, zd],
            sum_az_send.at[zd],
            sum_az_recv.at[way, zd],
            ahead[way],
        )

    def sum_bz(way, line, zd):
        return remote(
            zout_b.at[line, zd],
            zin_b.at[way, line, zd],
            sum_bz_send.at[line, zd],
            sum_bz_recv.at[way, line, zd],
            ahead[way],
        )

    def sum_by():
        return remote(yout_b, yin_b, sum_by_send, sum_by_recv, partner)

    def send_order(j):
        return nearness(z, 3 - lax.div(j, 2)), jnp.where(lax.rem(j, 2) == 0, other, y)

    def tile_chip(n):
        zd, line = send_order(n)
        m = n - 8
        zs = nearness(z, lax.div(m, 2))
        turn = jnp.where(lax.rem(m, 2) == 0, y, other)
        return jnp.where(n < 8, chip(zd, line), chip(zs, turn))

    def tile_copy(n):
        column = pl.multiple_of(tile_chip(n) * 2 * rows, 2 * rows)
        slot = lax.rem(n, 2)
        return pltpu.make_async_copy(
            target_ref.at[:, :, pl.ds(column, 2 * rows)], tiles.at[slot], tile_sem.at[slot]
        )

    def next_tile(n):
        @pl.when(n < 15)
        def _():
            tile_copy(n + 1).start()

        tile_copy(n).wait()

    fetch = pltpu.make_async_copy(record_ref, held, record_sem)
    fetch.start()
    tile_copy(0).start()
    here = chip(z, y)
    barrier = pltpu.get_barrier_semaphore()
    for device, there in (
        (sibling, None),
        (partner, None),
        (ahead[0], has_next[0]),
        (ahead[1], has_next[1]),
    ):

        def greet(device=device):
            pl.semaphore_signal(
                barrier, inc=1, device_id=(group, device), device_id_type=pl.DeviceIdType.MESH
            )

        if there is None:
            greet()
        else:
            pl.when(there)(greet)
    sample = lax.broadcasted_iota(jnp.int32, (WIDE, length), 0)
    column = lax.broadcasted_iota(jnp.int32, (WIDE, length), 1) - offset_ref[0]
    pick = jnp.where(column == sample, 1.0, 0.0).astype(jnp.bfloat16)
    fetch.wait()

    def cut(first, last):
        wins[here, k, first:last] = lax.dot_general(
            pick[first:last],
            held[...],
            (((1,), (1,)), ((), ())),
            preferred_element_type=jnp.float32,
        ).astype(jnp.bfloat16)

    cut(0, PART_A)
    pl.semaphore_wait(barrier, 2 + (z < 3).astype(jnp.int32) + (z > 0).astype(jnp.int32))
    for way in range(2):

        @pl.when(has_next[way])
        def _():
            win_az(way, z).start()

    cut(PART_A, WIDE)
    win_by(y).start()
    for way in range(2):

        @pl.when(has_next[way])
        def _():
            win_bz(way, y, z).start()

    win_sib(here, k).start()
    window = wins[here, k]

    own_ref[...] = jnp.zeros_like(own_ref)
    gram_ref[...] = jnp.zeros_like(gram_ref)
    flat_ref[:SAMPLES, :rows] = window[:SAMPLES]
    flat_ref[SAMPLES:, :rows] = jnp.zeros((WIDE - SAMPLES, rows), jnp.bfloat16)
    sample = lax.broadcasted_iota(jnp.int32, (WIDE, SAMPLES), 0)
    column = lax.broadcasted_iota(jnp.int32, (WIDE, SAMPLES), 1)
    pick = jnp.concatenate(
        [jnp.where(column + lag_ref[term] == sample, 1.0, 0.0) for term in range(LAGS)]
    ).astype(jnp.bfloat16)
    moved = jnp.dot(pick, window[:SAMPLES], preferred_element_type=jnp.float32)
    for term in range(LAGS):
        flat_ref[:, (1 + term) * rows : (2 + term) * rows] = moved[
            term * WIDE : (term + 1) * WIDE
        ].astype(jnp.bfloat16)

    def collect(j):
        zd, line = send_order(j)
        p = chip(zd, line)
        sum_sib(lax.rem(j, 2), p).wait_recv()
        parts[p] += sib_in[p]

        @pl.when(lax.rem(j, 2) == 0)
        def _():
            yout_a[zd] = parts[p, part_a].astype(jnp.bfloat16)

            @pl.when(j < 6)
            def _():
                sum_ay(zd).start()

    def relay_a(s, way):
        zs = z - sign[way] * s
        zd = z + sign[way] * (4 - s)

        @pl.when(first[way] >= s)
        def _():
            win_az(way, zs).wait_recv()

            @pl.when(has_next[way])
            def _():
                win_az(way, zs).start()

            win_ay(zs, y).start()

        return zd

    def forward_a(s, way):
        zd = z + sign[way] * (4 - s)

        @pl.when(first[way] < s)
        def _():
            sum_ay(zd).wait_recv()
            p = chip(zd, y)

            @pl.when(has_prev[way])
            def _():
                sum_az(way, zd).wait_recv()
                zout_a[zd] = (
                    parts[p, part_a]
                    + yin_a[zd].astype(jnp.float32)
                    + zin_a[way, zd].astype(jnp.float32)
                ).astype(jnp.bfloat16)

            @pl.when(jnp.logical_not(has_prev[way]))
            def _():
                zout_a[zd] = (parts[p, part_a] + yin_a[zd].astype(jnp.float32)).astype(
                    jnp.bfloat16
                )

            sum_az(way, zd).start()

    def relay_b(s, way, line):
        zs = z - sign[way] * s

        @pl.when(first[way] >= s)
        def _():
            win_bz(way, line, zs).wait_recv()

            @pl.when(has_next[way])
            def _():
                win_bz(way, line, zs).start()

    def share(s, way):
        zs = z - sign[way] * s

        @pl.when(first[way] >= s)
        def _():
            win_sib(chip(zs, y), k).start()

    def forward_b(s, way, line):
        zd = z + sign[way] * (4 - s)

        @pl.when(first[way] < s)
        def _():
            p = chip(zd, line)

            @pl.when(has_prev[way])
            def _():
                sum_bz(way, line, zd).wait_recv()
                zout_b[line, zd] = (
                    parts[p, part_b] + zin_b[way, line, zd].astype(jnp.float32)
                ).astype(jnp.bfloat16)

            @pl.when(jnp.logical_not(has_prev[way]))
            def _():
                zout_b[line, zd] = parts[p, part_b].astype(jnp.bfloat16)

            sum_bz(way, line, zd).start()

    def bracket(s, piece):
        for way in range(2):
            if piece == 0:
                relay_a(s, way)
                forward_b(s, way, other)
            elif piece == 1:
                relay_b(s, way, y)
                share(s, way)
                forward_a(s, way)
            else:
                relay_b(s, way, other)
                forward_b(s, way, y)

    def pass_on():
        win_by(other).wait_recv()
        for way in range(2):

            @pl.when(has_next[way])
            def _():
                win_bz(way, other, z).start()

    def finish_across():
        across = chip(z, other)
        for way in range(2):

            @pl.when(has_prev[way])
            def _():
                sum_bz(way, other, z).wait_recv()
                parts[across, part_b] += zin_b[way, other, z].astype(jnp.float32)

        yout_b[...] = parts[across, part_b].astype(jnp.bfloat16)
        sum_by().start()

    def at(step, table):
        for when, actions in table:

            @pl.when(step == when)
            def _():
                for action in actions:
                    action()

    def relay(s, piece):
        return lambda: bracket(s, piece)

    def send_step(j, carry):
        at(
            j,
            (
                (1, (lambda: win_ay(z, y).start(),)),
                (2, (pass_on,)),
                (3, (relay(1, 0),)),
                (5, (relay(1, 1),)),
                (6, (relay(1, 2),)),
                (7, (relay(2, 0),)),
            ),
        )
        next_tile(j)
        slot = lax.rem(j, 2)
        zd, line = send_order(j)
        p = chip(zd, line)

        @pl.when(j > 1)
        def _():
            sum_sib(slot, p).wait_send()

        def product(lane):
            column = pl.multiple_of(lane * rows, rows)
            tile = tiles[slot, :, :, pl.ds(column, rows)].reshape(TERMS * rows, rows)
            return jnp.dot(flat_ref[...], tile, preferred_element_type=jnp.float32)

        sib_out[slot] = product(1 - k)
        sum_sib(slot, p).start()
        parts[p] = product(k)

        @pl.when(j > 0)
        def _():
            collect(j - 1)

        return carry

    lax.fori_loop(0, 8, send_step, 0)
    bracket(2, 1)
    bracket(2, 2)
    collect(7)

    def use(n, p):
        next_tile(n)
        slot = lax.rem(n, 2)
        win_sib(p, 1 - k).wait_recv()
        window = jnp.concatenate([wins[p, 0], wins[p, 1]], axis=1)
        for term in range(TERMS):
            own_ref[term] += lax.dot_general(
                window,
                tiles[slot, term],
                (((1,), (1,)), ((), ())),
                preferred_element_type=jnp.float32,
            )

    def gram_copy():
        return remote(gram_ref, gram_in, gram_send, gram_recv, sibling)

    def open_round(rank):
        zs = nearness(z, rank)
        win_ay(zs, other).wait_recv()
        win_sib(chip(zs, other), k).start()
        pair = jnp.concatenate([wins[chip(zs, y), k], wins[chip(zs, other), k]], axis=1)
        gram_ref[...] += lax.dot_general(
            pair, pair, (((1,), (1,)), ((), ())), preferred_element_type=jnp.float32
        )

        @pl.when(rank == 3)
        def _():
            gram_copy().start()

    def use_step(n, carry):
        at(
            n,
            (
                (3, (relay(3, 0),)),
                (4, (lambda: sum_ay(z).start(),)),
                (5, (relay(3, 1),)),
                (6, (relay(3, 2), finish_across)),
            ),
        )
        rank = lax.div(n, 2)

        @pl.when(lax.rem(n, 2) == 0)
        def _():
            open_round(rank)

        use(8 + n, chip(nearness(z, rank), jnp.where(lax.rem(n, 2) == 0, y, other)))
        return carry

    lax.fori_loop(0, 8, use_step, 0)

    gram_copy().wait_recv()
    gram = jnp.concatenate(
        [gram_ref[...] + gram_in[...], jnp.zeros((WIDE, WIDTH - WIDE), jnp.float32)], axis=1
    )
    inside = (lax.broadcasted_iota(jnp.int32, gram.shape, 0) < SAMPLES) & (
        lax.broadcasted_iota(jnp.int32, gram.shape, 1) < SAMPLES
    )
    early_gram = jnp.where(inside, gram, 0.0)
    before = 2.0 * gram
    after = jnp.zeros_like(gram)
    early = own_ref[0, :SAMPLES]
    for term in range(LAGS):
        lag = lag_ref[term]
        before += pltpu.roll(pltpu.roll(gram, WIDE - lag, 0), WIDTH - lag, 1)
        after += pltpu.roll(pltpu.roll(early_gram, lag, 0), lag, 1)
        moved = own_ref[1 + term, 1:SPAN]
        for step in (4, 2, 1):
            size = moved.shape[0] - step
            moved = jnp.where(((lag - 1) & step) > 0, moved[step:], moved[:size])
        early = early + moved
    mixed = (jnp.where(inside, before, 0.0) + after)[:, :WIDE]
    coarse = mixed.astype(jnp.bfloat16)
    fine = (mixed - coarse.astype(jnp.float32)).astype(jnp.bfloat16)
    window = wins[here, k]
    smooth = jnp.dot(coarse, window, preferred_element_type=jnp.float32) + jnp.dot(
        fine, window, preferred_element_type=jnp.float32
    )
    base_ref[...] = smooth * (1.0 / regions) - weight * parts[here]
    base_ref[:SAMPLES] -= weight * early

    sum_ay(z).wait_recv()
    base_ref[part_a] -= weight * yin_a[z].astype(jnp.float32)
    for way in range(2):

        @pl.when(has_prev[way])
        def _():
            sum_az(way, z).wait_recv()
            base_ref[part_a] -= weight * zin_a[way, z].astype(jnp.float32)

    sum_by().wait_recv()
    base_ref[part_b] -= weight * yin_b[...].astype(jnp.float32)
    for way in range(2):

        @pl.when(has_prev[way])
        def _():
            sum_bz(way, y, z).wait_recv()
            base_ref[part_b] -= weight * zin_b[way, y, z].astype(jnp.float32)

    def give(slab):
        lines = pl.ds(slab * SLAB, SLAB)
        return pltpu.make_async_copy(
            result.at[lines], grad_ref.at[lines], grad_sem.at[slab]
        )

    for slab in range(rows // SLAB):
        lines = slice(slab * SLAB, (slab + 1) * SLAB)
        turned = jnp.concatenate(
            [base_ref[:, lines].T, jnp.zeros((SLAB, length - WIDE), jnp.float32)], axis=1
        )
        result[lines] = pltpu.roll(turned, offset_ref[0], 1)
        give(slab).start()
    for slab in range(rows // SLAB):
        give(slab).wait()

    gram_copy().wait_send()
    win_by(y).wait_send()
    sum_by().wait_send()
    for slot in range(2):
        sum_sib(slot, here).wait_send()

    def drain(i, carry):
        win_ay(i, y).wait_send()
        sum_ay(i).wait_send()
        for line in range(2):
            win_sib(chip(i, line), k).wait_send()
        for way in range(2):
            reached = (i <= z, i >= z)[way]
            beyond = (i > z, i < z)[way]

            @pl.when(reached & has_next[way])
            def _():
                win_az(way, i).wait_send()
                for line in range(2):
                    win_bz(way, line, i).wait_send()

            @pl.when(beyond)
            def _():
                sum_az(way, i).wait_send()
                for line in range(2):
                    sum_bz(way, line, i).wait_send()

        return carry

    lax.fori_loop(0, 4, drain, 0)


def mesh_shards(record, target, offset, lag_steps):
    rows, length = record.shape
    regions = target.shape[2]
    rest = WIDE - PART_A
    work = 4 * TERMS * rows * regions * WIDE
    dma = pltpu.SemaphoreType.DMA
    half, full = jnp.bfloat16, jnp.float32
    smem = pl.BlockSpec(memory_space=pltpu.SMEM)
    return pl.pallas_call(
        mesh_kernel,
        in_specs=[smem, smem] + [pl.BlockSpec(memory_space=pl.ANY)] * 2,
        out_specs=pl.BlockSpec(memory_space=pl.ANY),
        out_shape=jax.ShapeDtypeStruct((rows, length), full),
        scratch_shapes=[
            pltpu.VMEM((WIDE, TERMS * rows), half),
            pltpu.VMEM((TERMS, WIDE, rows), full),
            pltpu.VMEM((WIDE, WIDE), full),
            pltpu.VMEM((WIDE, WIDE), full),
            pltpu.VMEM((WIDE, rows), full),
            pltpu.VMEM((rows, length), half),
            pltpu.VMEM((rows, length), full),
            pltpu.VMEM((8, 2, WIDE, rows), half),
            pltpu.VMEM((2, TERMS, rows, 2 * rows), half),
            pltpu.VMEM((8, WIDE, rows), full),
            pltpu.VMEM((8, WIDE, rows), full),
            pltpu.VMEM((2, WIDE, rows), full),
            pltpu.VMEM((4, PART_A, rows), half),
            pltpu.VMEM((rest, rows), half),
            pltpu.VMEM((4, PART_A, rows), half),
            pltpu.VMEM((rest, rows), half),
            pltpu.VMEM((2, 4, PART_A, rows), half),
            pltpu.VMEM((2, 2, 4, rest, rows), half),
            pltpu.VMEM((4, PART_A, rows), half),
            pltpu.VMEM((2, 4, rest, rows), half),
            dma,
            dma((rows // SLAB,)),
            dma((2,)),
            dma((8,)),
            dma((8,)),
            dma((2, 4)),
            dma((4,)),
            dma((4,)),
            dma((4,)),
            dma,
            dma,
            dma((2, 2, 4)),
            dma((2, 4)),
            dma((2,)),
            dma((8,)),
            dma((4,)),
            dma((4,)),
            dma((4,)),
            dma((2, 4)),
            dma((2, 4)),
            dma((2, 2, 4)),
            dma,
            dma,
            dma,
            dma,
        ],
        compiler_params=pltpu.CompilerParams(
            collective_id=0, has_side_effects=True, vmem_limit_bytes=60 << 20
        ),
        cost_estimate=pl.CostEstimate(flops=work, bytes_accessed=70 << 20, transcendentals=0),
        name="mesh",
    )(offset, lag_steps, record, target)


def gather_call(regions, devices, scaled, flat, turned, target):
    rows = target.shape[1]
    gathered = lax.all_gather(turned, "region")
    blocks = regions // WIDTH
    if rows != WIDTH:
        gathered = (
            gathered.reshape(blocks, WIDTH // rows, WIDE, rows)
            .transpose(0, 2, 1, 3)
            .reshape(blocks, WIDE, WIDTH)
        )
    partials, own = pl.pallas_call(
        lambda *refs: block_kernel(SAMPLES / regions, *refs),
        grid=(blocks,),
        in_specs=[
            pl.BlockSpec((TERMS, rows, WIDE), lambda i: (0, 0, 0)),
            pl.BlockSpec((SPAN, TERMS * rows), lambda i: (0, 0)),
            pl.BlockSpec((1, WIDE, WIDTH), lambda i: (i, 0, 0)),
            pl.BlockSpec((TERMS, rows, WIDTH), lambda i: (0, 0, i)),
        ],
        out_specs=[
            pl.BlockSpec((1, SPAN, WIDTH), lambda i: (i, 0, 0)),
            pl.BlockSpec((TERMS, WIDE, rows), lambda i: (0, 0, 0)),
        ],
        out_shape=[
            jax.ShapeDtypeStruct((blocks, SPAN, WIDTH), jnp.float32),
            jax.ShapeDtypeStruct((TERMS, WIDE, rows), jnp.float32),
        ],
        compiler_params=pltpu.CompilerParams(vmem_limit_bytes=56 << 20),
        name="blocks",
    )(scaled, flat, gathered, target)
    if rows != WIDTH:
        partials = (
            partials.reshape(blocks, SPAN, WIDTH // rows, rows)
            .transpose(0, 2, 1, 3)
            .reshape(devices, SPAN, rows)
        )
    summed = lax.psum_scatter(partials, "region", scatter_dimension=0, tiled=True)[0]
    return summed, own


def shards(record, target, offset, lag_steps):
    rows = record.shape[0]
    regions = target.shape[2]
    devices = lax.axis_size("region")
    if rows == WIDTH and devices == 16:
        return mesh_shards(record, target, offset, lag_steps)
    begin_at = offset[0]
    window = lax.dynamic_slice_in_dim(record, begin_at, WIDE, 1)
    stacked, shifts = placed_early(window[:, :SAMPLES], lag_steps)
    scaled = stacked * jnp.bfloat16(1.0 / regions)
    flat = stacked[:, :, :SPAN].transpose(2, 0, 1).reshape(SPAN, TERMS * rows)
    turned = window.T
    summed, own = gather_call(regions, devices, scaled, flat, turned, target)
    early = None
    for term in range(TERMS):
        part = lax.dynamic_slice(own[term], (shifts[term], 0), (SAMPLES, rows))
        early = part if early is None else early + part
    in_window = summed + jnp.pad(early, ((0, MAXLAG), (0, 0)))
    grad = jnp.zeros((record.shape[1], rows), jnp.float32)
    return lax.dynamic_update_slice(grad, in_window, (begin_at, 0)).T


def solution(mesh):
    placed = (
        P(("groups", "region"), None),
        P(None, ("groups", "region"), None),
        P("groups"),
        P("groups"),
    )
    return jax.shard_map(
        shards, mesh=mesh, in_specs=placed, out_specs=P(("groups", "region"), None), check_vma=False
    )
```

```python
import jax
import jax.numpy as jnp
from jax import lax
from jax.experimental import pallas as pl
from jax.experimental.pallas import tpu as pltpu
from jax.sharding import PartitionSpec as P

SAMPLES = 384
MAXLAG = 8
LAGS = 3
TERMS = 1 + LAGS
WIDE = 400
SPAN = SAMPLES + MAXLAG
WIDTH = 512
PART_A = 240
SLAB = 128


def placed_early(early, lag_steps):
    rows = early.shape[0]
    shifts = jnp.concatenate([jnp.zeros((1,), jnp.int32), lag_steps])
    padded = jnp.pad(early, ((0, 0), (MAXLAG, WIDE - SAMPLES)))
    parts = [
        lax.dynamic_slice(padded, (0, MAXLAG - shifts[term]), (rows, WIDE)) for term in range(TERMS)
    ]
    return jnp.stack(parts), shifts


def block_kernel(weight, scaled_ref, flat_ref, window_ref, target_ref, partial_ref, own_ref):
    rows = target_ref.shape[1]

    @pl.when(pl.program_id(0) == 0)
    def _():
        own_ref[...] = jnp.zeros_like(own_ref)

    window = window_ref[0]
    total = None
    for term in range(TERMS):
        cov = jnp.dot(scaled_ref[term], window, preferred_element_type=jnp.float32)
        error = (cov - weight * target_ref[term].astype(jnp.float32)).astype(jnp.bfloat16)
        own_ref[term] += lax.dot_general(
            window, error, (((1,), (1,)), ((), ())), preferred_element_type=jnp.float32
        )
        part = jnp.dot(
            flat_ref[:, term * rows : (term + 1) * rows], error, preferred_element_type=jnp.float32
        )
        total = part if total is None else total + part
    partial_ref[0] = total


def nearness(z, rank):
    low = jnp.minimum(z, 3 - z)
    seen = jnp.where((low == 1) & (rank < 2), 1 - rank, rank)
    return jnp.where(z < 2, seen, 3 - seen)


def mesh_kernel(
    offset_hbm,
    lag_hbm,
    record_ref,
    target_ref,
    grad_ref,
    flat_ref,
    own_ref,
    gram_ref,
    gram_in,
    base_ref,
    offset_ref,
    lag_ref,
    held,
    result,
    wins,
    tiles,
    parts,
    sib_in,
    sib_out,
    yin_a,
    yin_b,
    yout_a,
    yout_b,
    zin_a,
    zin_b,
    zout_a,
    zout_b,
    offset_sem,
    lag_sem,
    record_sem,
    grad_sem,
    tile_sem,
    win_sib_send,
    win_sib_recv,
    win_az_send,
    win_az_recv,
    win_ay_send,
    win_ay_recv,
    win_by_send,
    win_by_recv,
    win_bz_send,
    win_bz_recv,
    sum_sib_send,
    sum_sib_recv,
    sum_ay_send,
    sum_ay_recv,
    sum_az_send,
    sum_az_recv,
    sum_bz_send,
    sum_bz_recv,
    sum_by_send,
    sum_by_recv,
    gram_send,
    gram_recv,
):
    rows, length = record_ref.shape
    regions = target_ref.shape[2]
    weight = SAMPLES / regions
    group = lax.axis_index("groups")
    region = lax.axis_index("region")
    z = lax.div(region, 4)
    y = lax.rem(lax.div(region, 2), 2)
    k = lax.rem(region, 2)
    other = 1 - y
    sibling = 4 * z + 2 * y + 1 - k
    partner = 4 * z + 2 * other + k
    ahead = (region + 4, region - 4)
    has_next = (z < 3, z > 0)
    has_prev = (z > 0, z < 3)
    sign = (1, -1)
    first = (z, 3 - z)
    part_a = pl.ds(0, PART_A)
    part_b = pl.ds(PART_A, WIDE - PART_A)

    def chip(zz, yy):
        return 2 * zz + yy

    def remote(src, dst, send, recv, device):
        return pltpu.make_async_remote_copy(
            src_ref=src,
            dst_ref=dst,
            send_sem=send,
            recv_sem=recv,
            device_id=(group, device),
            device_id_type=pl.DeviceIdType.MESH,
        )

    def win_sib(p, lane):
        ref = wins.at[p, lane]
        return remote(ref, ref, win_sib_send.at[p], win_sib_recv.at[p], sibling)

    def win_az(way, zs):
        ref = wins.at[chip(zs, y), k, part_a]
        return remote(ref, ref, win_az_send.at[way, zs], win_az_recv.at[zs], ahead[way])

    def win_ay(zs, line):
        ref = wins.at[chip(zs, line), k, part_a]
        return remote(ref, ref, win_ay_send.at[zs], win_ay_recv.at[zs], partner)

    def win_by(line):
        ref = wins.at[chip(z, line), k, part_b]
        return remote(ref, ref, win_by_send, win_by_recv, partner)

    def win_bz(way, line, zs):
        ref = wins.at[chip(zs, line), k, part_b]
        return remote(
            ref, ref, win_bz_send.at[way, line, zs], win_bz_recv.at[line, zs], ahead[way]
        )

    def sum_sib(slot, p):
        return remote(
            sib_out.at[slot], sib_in.at[p], sum_sib_send.at[slot], sum_sib_recv.at[p], sibling
        )

    def sum_ay(zd):
        return remote(yout_a.at[zd], yin_a.at[zd], sum_ay_send.at[zd], sum_ay_recv.at[zd], partner)

    def sum_az(way, zd):
        return remote(
            zout_a.at[zd],
            zin_a.at[way, zd],
            sum_az_send.at[zd],
            sum_az_recv.at[way, zd],
            ahead[way],
        )

    def sum_bz(way, line, zd):
        return remote(
            zout_b.at[line, zd],
            zin_b.at[way, line, zd],
            sum_bz_send.at[line, zd],
            sum_bz_recv.at[way, line, zd],
            ahead[way],
        )

    def sum_by():
        return remote(yout_b, yin_b, sum_by_send, sum_by_recv, partner)

    def send_order(j):
        return nearness(z, 3 - lax.div(j, 2)), jnp.where(lax.rem(j, 2) == 0, other, y)

    def tile_chip(n):
        zd, line = send_order(n)
        m = n - 8
        zs = nearness(z, lax.div(m, 2))
        turn = jnp.where(lax.rem(m, 2) == 0, y, other)
        return jnp.where(n < 8, chip(zd, line), chip(zs, turn))

    def tile_copy(n):
        column = pl.multiple_of(tile_chip(n) * 2 * rows, 2 * rows)
        slot = lax.rem(n, 2)
        return pltpu.make_async_copy(
            target_ref.at[:, :, pl.ds(column, 2 * rows)], tiles.at[slot], tile_sem.at[slot]
        )

    def next_tile(n):
        @pl.when(n < 15)
        def _():
            tile_copy(n + 1).start()

        tile_copy(n).wait()

    fetch = pltpu.make_async_copy(record_ref, held, record_sem)
    fetch_offset = pltpu.make_async_copy(offset_hbm, offset_ref, offset_sem)
    fetch_lag = pltpu.make_async_copy(lag_hbm, lag_ref, lag_sem)
    fetch_offset.start()
    fetch.start()
    fetch_lag.start()
    tile_copy(0).start()
    here = chip(z, y)
    barrier = pltpu.get_barrier_semaphore()
    for device, there in (
        (sibling, None),
        (partner, None),
        (ahead[0], has_next[0]),
        (ahead[1], has_next[1]),
    ):

        def greet(device=device):
            pl.semaphore_signal(
                barrier, inc=1, device_id=(group, device), device_id_type=pl.DeviceIdType.MESH
            )

        if there is None:
            greet()
        else:
            pl.when(there)(greet)
    fetch_offset.wait()
    fetch_lag.wait()
    sample = lax.broadcasted_iota(jnp.int32, (WIDE, length), 0)
    column = lax.broadcasted_iota(jnp.int32, (WIDE, length), 1) - offset_ref[0]
    pick = jnp.where(column == sample, 1.0, 0.0).astype(jnp.bfloat16)
    fetch.wait()

    def cut(first, last):
        wins[here, k, first:last] = lax.dot_general(
            pick[first:last],
            held[...],
            (((1,), (1,)), ((), ())),
            preferred_element_type=jnp.float32,
        ).astype(jnp.bfloat16)

    cut(0, PART_A)
    pl.semaphore_wait(barrier, 2 + (z < 3).astype(jnp.int32) + (z > 0).astype(jnp.int32))
    for way in range(2):

        @pl.when(has_next[way])
        def _():
            win_az(way, z).start()

    cut(PART_A, WIDE)
    win_by(y).start()
    for way in range(2):

        @pl.when(has_next[way])
        def _():
            win_bz(way, y, z).start()

    win_sib(here, k).start()
    window = wins[here, k]

    own_ref[...] = jnp.zeros_like(own_ref)
    gram_ref[...] = jnp.zeros_like(gram_ref)
    flat_ref[:SAMPLES, :rows] = window[:SAMPLES]
    flat_ref[SAMPLES:, :rows] = jnp.zeros((WIDE - SAMPLES, rows), jnp.bfloat16)
    sample = lax.broadcasted_iota(jnp.int32, (WIDE, SAMPLES), 0)
    column = lax.broadcasted_iota(jnp.int32, (WIDE, SAMPLES), 1)
    pick = jnp.concatenate(
        [jnp.where(column + lag_ref[term] == sample, 1.0, 0.0) for term in range(LAGS)]
    ).astype(jnp.bfloat16)
    moved = jnp.dot(pick, window[:SAMPLES], preferred_element_type=jnp.float32)
    for term in range(LAGS):
        flat_ref[:, (1 + term) * rows : (2 + term) * rows] = moved[
            term * WIDE : (term + 1) * WIDE
        ].astype(jnp.bfloat16)

    def collect(j):
        zd, line = send_order(j)
        p = chip(zd, line)
        sum_sib(lax.rem(j, 2), p).wait_recv()
        parts[p] += sib_in[p]

        @pl.when(lax.rem(j, 2) == 0)
        def _():
            yout_a[zd] = parts[p, part_a].astype(jnp.bfloat16)

            @pl.when(j < 6)
            def _():
                sum_ay(zd).start()

    def relay_a(s, way):
        zs = z - sign[way] * s
        zd = z + sign[way] * (4 - s)

        @pl.when(first[way] >= s)
        def _():
            win_az(way, zs).wait_recv()

            @pl.when(has_next[way])
            def _():
                win_az(way, zs).start()

            win_ay(zs, y).start()

        return zd

    def forward_a(s, way):
        zd = z + sign[way] * (4 - s)

        @pl.when(first[way] < s)
        def _():
            sum_ay(zd).wait_recv()
            p = chip(zd, y)

            @pl.when(has_prev[way])
            def _():
                sum_az(way, zd).wait_recv()
                zout_a[zd] = (
                    parts[p, part_a]
                    + yin_a[zd].astype(jnp.float32)
                    + zin_a[way, zd].astype(jnp.float32)
                ).astype(jnp.bfloat16)

            @pl.when(jnp.logical_not(has_prev[way]))
            def _():
                zout_a[zd] = (parts[p, part_a] + yin_a[zd].astype(jnp.float32)).astype(
                    jnp.bfloat16
                )

            sum_az(way, zd).start()

    def relay_b(s, way, line):
        zs = z - sign[way] * s

        @pl.when(first[way] >= s)
        def _():
            win_bz(way, line, zs).wait_recv()

            @pl.when(has_next[way])
            def _():
                win_bz(way, line, zs).start()

    def share(s, way):
        zs = z - sign[way] * s

        @pl.when(first[way] >= s)
        def _():
            win_sib(chip(zs, y), k).start()

    def forward_b(s, way, line):
        zd = z + sign[way] * (4 - s)

        @pl.when(first[way] < s)
        def _():
            p = chip(zd, line)

            @pl.when(has_prev[way])
            def _():
                sum_bz(way, line, zd).wait_recv()
                zout_b[line, zd] = (
                    parts[p, part_b] + zin_b[way, line, zd].astype(jnp.float32)
                ).astype(jnp.bfloat16)

            @pl.when(jnp.logical_not(has_prev[way]))
            def _():
                zout_b[line, zd] = parts[p, part_b].astype(jnp.bfloat16)

            sum_bz(way, line, zd).start()

    def bracket(s, piece):
        for way in range(2):
            if piece == 0:
                relay_a(s, way)
                forward_b(s, way, other)
            elif piece == 1:
                relay_b(s, way, y)
                share(s, way)
                forward_a(s, way)
            else:
                relay_b(s, way, other)
                forward_b(s, way, y)

    def pass_on():
        win_by(other).wait_recv()
        for way in range(2):

            @pl.when(has_next[way])
            def _():
                win_bz(way, other, z).start()

    def finish_across():
        across = chip(z, other)
        for way in range(2):

            @pl.when(has_prev[way])
            def _():
                sum_bz(way, other, z).wait_recv()
                parts[across, part_b] += zin_b[way, other, z].astype(jnp.float32)

        yout_b[...] = parts[across, part_b].astype(jnp.bfloat16)
        sum_by().start()

    def at(step, table):
        for when, actions in table:

            @pl.when(step == when)
            def _():
                for action in actions:
                    action()

    def relay(s, piece):
        return lambda: bracket(s, piece)

    def send_step(j, carry):
        at(
            j,
            (
                (1, (lambda: win_ay(z, y).start(),)),
                (2, (pass_on,)),
                (3, (relay(1, 0),)),
                (5, (relay(1, 1),)),
                (6, (relay(1, 2),)),
                (7, (relay(2, 0),)),
            ),
        )
        next_tile(j)
        slot = lax.rem(j, 2)
        zd, line = send_order(j)
        p = chip(zd, line)

        @pl.when(j > 1)
        def _():
            sum_sib(slot, p).wait_send()

        def product(lane):
            column = pl.multiple_of(lane * rows, rows)
            tile = tiles[slot, :, :, pl.ds(column, rows)].reshape(TERMS * rows, rows)
            return jnp.dot(flat_ref[...], tile, preferred_element_type=jnp.float32)

        sib_out[slot] = product(1 - k)
        sum_sib(slot, p).start()
        parts[p] = product(k)

        @pl.when(j > 0)
        def _():
            collect(j - 1)

        return carry

    lax.fori_loop(0, 8, send_step, 0)
    bracket(2, 1)
    bracket(2, 2)
    collect(7)

    def use(n, p):
        next_tile(n)
        slot = lax.rem(n, 2)
        win_sib(p, 1 - k).wait_recv()
        window = jnp.concatenate([wins[p, 0], wins[p, 1]], axis=1)
        for term in range(TERMS):
            own_ref[term] += lax.dot_general(
                window,
                tiles[slot, term],
                (((1,), (1,)), ((), ())),
                preferred_element_type=jnp.float32,
            )

    def gram_copy():
        return remote(gram_ref, gram_in, gram_send, gram_recv, sibling)

    def open_round(rank):
        zs = nearness(z, rank)
        win_ay(zs, other).wait_recv()
        win_sib(chip(zs, other), k).start()
        pair = jnp.concatenate([wins[chip(zs, y), k], wins[chip(zs, other), k]], axis=1)
        gram_ref[...] += lax.dot_general(
            pair, pair, (((1,), (1,)), ((), ())), preferred_element_type=jnp.float32
        )

        @pl.when(rank == 3)
        def _():
            gram_copy().start()

    def use_step(n, carry):
        at(
            n,
            (
                (3, (relay(3, 0),)),
                (4, (lambda: sum_ay(z).start(),)),
                (5, (relay(3, 1),)),
                (6, (relay(3, 2), finish_across)),
            ),
        )
        rank = lax.div(n, 2)

        @pl.when(lax.rem(n, 2) == 0)
        def _():
            open_round(rank)

        use(8 + n, chip(nearness(z, rank), jnp.where(lax.rem(n, 2) == 0, y, other)))
        return carry

    lax.fori_loop(0, 8, use_step, 0)

    gram_copy().wait_recv()
    gram = jnp.concatenate(
        [gram_ref[...] + gram_in[...], jnp.zeros((WIDE, WIDTH - WIDE), jnp.float32)], axis=1
    )
    inside = (lax.broadcasted_iota(jnp.int32, gram.shape, 0) < SAMPLES) & (
        lax.broadcasted_iota(jnp.int32, gram.shape, 1) < SAMPLES
    )
    early_gram = jnp.where(inside, gram, 0.0)
    before = 2.0 * gram
    after = jnp.zeros_like(gram)
    early = own_ref[0, :SAMPLES]
    for term in range(LAGS):
        lag = lag_ref[term]
        before += pltpu.roll(pltpu.roll(gram, WIDE - lag, 0), WIDTH - lag, 1)
        after += pltpu.roll(pltpu.roll(early_gram, lag, 0), lag, 1)
        moved = own_ref[1 + term, 1:SPAN]
        for step in (4, 2, 1):
            size = moved.shape[0] - step
            moved = jnp.where(((lag - 1) & step) > 0, moved[step:], moved[:size])
        early = early + moved
    mixed = (jnp.where(inside, before, 0.0) + after)[:, :WIDE]
    coarse = mixed.astype(jnp.bfloat16)
    fine = (mixed - coarse.astype(jnp.float32)).astype(jnp.bfloat16)
    window = wins[here, k]
    smooth = jnp.dot(coarse, window, preferred_element_type=jnp.float32) + jnp.dot(
        fine, window, preferred_element_type=jnp.float32
    )
    base_ref[...] = smooth * (1.0 / regions) - weight * parts[here]
    base_ref[:SAMPLES] -= weight * early

    sum_ay(z).wait_recv()
    base_ref[part_a] -= weight * yin_a[z].astype(jnp.float32)
    for way in range(2):

        @pl.when(has_prev[way])
        def _():
            sum_az(way, z).wait_recv()
            base_ref[part_a] -= weight * zin_a[way, z].astype(jnp.float32)

    sum_by().wait_recv()
    base_ref[part_b] -= weight * yin_b[...].astype(jnp.float32)
    for way in range(2):

        @pl.when(has_prev[way])
        def _():
            sum_bz(way, y, z).wait_recv()
            base_ref[part_b] -= weight * zin_b[way, y, z].astype(jnp.float32)

    def give(slab):
        lines = pl.ds(slab * SLAB, SLAB)
        return pltpu.make_async_copy(
            result.at[lines], grad_ref.at[lines], grad_sem.at[slab]
        )

    for slab in range(rows // SLAB):
        lines = slice(slab * SLAB, (slab + 1) * SLAB)
        turned = jnp.concatenate(
            [base_ref[:, lines].T, jnp.zeros((SLAB, length - WIDE), jnp.float32)], axis=1
        )
        result[lines] = pltpu.roll(turned, offset_ref[0], 1)
        give(slab).start()
    for slab in range(rows // SLAB):
        give(slab).wait()

    gram_copy().wait_send()
    win_by(y).wait_send()
    sum_by().wait_send()
    for slot in range(2):
        sum_sib(slot, here).wait_send()

    def drain(i, carry):
        win_ay(i, y).wait_send()
        sum_ay(i).wait_send()
        for line in range(2):
            win_sib(chip(i, line), k).wait_send()
        for way in range(2):
            reached = (i <= z, i >= z)[way]
            beyond = (i > z, i < z)[way]

            @pl.when(reached & has_next[way])
            def _():
                win_az(way, i).wait_send()
                for line in range(2):
                    win_bz(way, line, i).wait_send()

            @pl.when(beyond)
            def _():
                sum_az(way, i).wait_send()
                for line in range(2):
                    sum_bz(way, line, i).wait_send()

        return carry

    lax.fori_loop(0, 4, drain, 0)


def mesh_shards(record, target, offset, lag_steps):
    rows, length = record.shape
    regions = target.shape[2]
    rest = WIDE - PART_A
    work = 4 * TERMS * rows * regions * WIDE
    dma = pltpu.SemaphoreType.DMA
    half, full = jnp.bfloat16, jnp.float32
    return pl.pallas_call(
        mesh_kernel,
        in_specs=[pl.BlockSpec(memory_space=pl.ANY)] * 4,
        out_specs=pl.BlockSpec(memory_space=pl.ANY),
        out_shape=jax.ShapeDtypeStruct((rows, length), full),
        scratch_shapes=[
            pltpu.VMEM((WIDE, TERMS * rows), half),
            pltpu.VMEM((TERMS, WIDE, rows), full),
            pltpu.VMEM((WIDE, WIDE), full),
            pltpu.VMEM((WIDE, WIDE), full),
            pltpu.VMEM((WIDE, rows), full),
            pltpu.SMEM((1,), jnp.int32),
            pltpu.SMEM((LAGS,), jnp.int32),
            pltpu.VMEM((rows, length), half),
            pltpu.VMEM((rows, length), full),
            pltpu.VMEM((8, 2, WIDE, rows), half),
            pltpu.VMEM((2, TERMS, rows, 2 * rows), half),
            pltpu.VMEM((8, WIDE, rows), full),
            pltpu.VMEM((8, WIDE, rows), full),
            pltpu.VMEM((2, WIDE, rows), full),
            pltpu.VMEM((4, PART_A, rows), half),
            pltpu.VMEM((rest, rows), half),
            pltpu.VMEM((4, PART_A, rows), half),
            pltpu.VMEM((rest, rows), half),
            pltpu.VMEM((2, 4, PART_A, rows), half),
            pltpu.VMEM((2, 2, 4, rest, rows), half),
            pltpu.VMEM((4, PART_A, rows), half),
            pltpu.VMEM((2, 4, rest, rows), half),
            dma,
            dma,
            dma,
            dma((rows // SLAB,)),
            dma((2,)),
            dma((8,)),
            dma((8,)),
            dma((2, 4)),
            dma((4,)),
            dma((4,)),
            dma((4,)),
            dma,
            dma,
            dma((2, 2, 4)),
            dma((2, 4)),
            dma((2,)),
            dma((8,)),
            dma((4,)),
            dma((4,)),
            dma((4,)),
            dma((2, 4)),
            dma((2, 4)),
            dma((2, 2, 4)),
            dma,
            dma,
            dma,
            dma,
        ],
        compiler_params=pltpu.CompilerParams(
            collective_id=0, has_side_effects=True, vmem_limit_bytes=60 << 20
        ),
        cost_estimate=pl.CostEstimate(flops=work, bytes_accessed=70 << 20, transcendentals=0),
        name="mesh",
    )(offset, lag_steps, record, target)


def gather_call(regions, devices, scaled, flat, turned, target):
    rows = target.shape[1]
    gathered = lax.all_gather(turned, "region")
    blocks = regions // WIDTH
    if rows != WIDTH:
        gathered = (
            gathered.reshape(blocks, WIDTH // rows, WIDE, rows)
            .transpose(0, 2, 1, 3)
            .reshape(blocks, WIDE, WIDTH)
        )
    partials, own = pl.pallas_call(
        lambda *refs: block_kernel(SAMPLES / regions, *refs),
        grid=(blocks,),
        in_specs=[
            pl.BlockSpec((TERMS, rows, WIDE), lambda i: (0, 0, 0)),
            pl.BlockSpec((SPAN, TERMS * rows), lambda i: (0, 0)),
            pl.BlockSpec((1, WIDE, WIDTH), lambda i: (i, 0, 0)),
            pl.BlockSpec((TERMS, rows, WIDTH), lambda i: (0, 0, i)),
        ],
        out_specs=[
            pl.BlockSpec((1, SPAN, WIDTH), lambda i: (i, 0, 0)),
            pl.BlockSpec((TERMS, WIDE, rows), lambda i: (0, 0, 0)),
        ],
        out_shape=[
            jax.ShapeDtypeStruct((blocks, SPAN, WIDTH), jnp.float32),
            jax.ShapeDtypeStruct((TERMS, WIDE, rows), jnp.float32),
        ],
        compiler_params=pltpu.CompilerParams(vmem_limit_bytes=56 << 20),
        name="blocks",
    )(scaled, flat, gathered, target)
    if rows != WIDTH:
        partials = (
            partials.reshape(blocks, SPAN, WIDTH // rows, rows)
            .transpose(0, 2, 1, 3)
            .reshape(devices, SPAN, rows)
        )
    summed = lax.psum_scatter(partials, "region", scatter_dimension=0, tiled=True)[0]
    return summed, own


def shards(record, target, offset, lag_steps):
    rows = record.shape[0]
    regions = target.shape[2]
    devices = lax.axis_size("region")
    if rows == WIDTH and devices == 16:
        return mesh_shards(record, target, offset, lag_steps)
    begin_at = offset[0]
    window = lax.dynamic_slice_in_dim(record, begin_at, WIDE, 1)
    stacked, shifts = placed_early(window[:, :SAMPLES], lag_steps)
    scaled = stacked * jnp.bfloat16(1.0 / regions)
    flat = stacked[:, :, :SPAN].transpose(2, 0, 1).reshape(SPAN, TERMS * rows)
    turned = window.T
    summed, own = gather_call(regions, devices, scaled, flat, turned, target)
    early = None
    for term in range(TERMS):
        part = lax.dynamic_slice(own[term], (shifts[term], 0), (SAMPLES, rows))
        early = part if early is None else early + part
    in_window = summed + jnp.pad(early, ((0, MAXLAG), (0, 0)))
    grad = jnp.zeros((record.shape[1], rows), jnp.float32)
    return lax.dynamic_update_slice(grad, in_window, (begin_at, 0)).T


def solution(mesh):
    placed = (
        P(("groups", "region"), None),
        P(None, ("groups", "region"), None),
        P("groups"),
        P("groups"),
    )
    return jax.shard_map(
        shards, mesh=mesh, in_specs=placed, out_specs=P(("groups", "region"), None), check_vma=False
    )
```

```python
import jax
import jax.numpy as jnp
from jax import lax
from jax.experimental import pallas as pl
from jax.experimental.pallas import tpu as pltpu
from jax.sharding import PartitionSpec as P

SAMPLES = 384
MAXLAG = 8
LAGS = 3
TERMS = 1 + LAGS
WIDE = 400
SPAN = SAMPLES + MAXLAG
WIDTH = 512
PART_A = 240
SLAB = 128


def placed_early(early, lag_steps):
    rows = early.shape[0]
    shifts = jnp.concatenate([jnp.zeros((1,), jnp.int32), lag_steps])
    padded = jnp.pad(early, ((0, 0), (MAXLAG, WIDE - SAMPLES)))
    parts = [
        lax.dynamic_slice(padded, (0, MAXLAG - shifts[term]), (rows, WIDE)) for term in range(TERMS)
    ]
    return jnp.stack(parts), shifts


def block_kernel(weight, scaled_ref, flat_ref, window_ref, target_ref, partial_ref, own_ref):
    rows = target_ref.shape[1]

    @pl.when(pl.program_id(0) == 0)
    def _():
        own_ref[...] = jnp.zeros_like(own_ref)

    window = window_ref[0]
    total = None
    for term in range(TERMS):
        cov = jnp.dot(scaled_ref[term], window, preferred_element_type=jnp.float32)
        error = (cov - weight * target_ref[term].astype(jnp.float32)).astype(jnp.bfloat16)
        own_ref[term] += lax.dot_general(
            window, error, (((1,), (1,)), ((), ())), preferred_element_type=jnp.float32
        )
        part = jnp.dot(
            flat_ref[:, term * rows : (term + 1) * rows], error, preferred_element_type=jnp.float32
        )
        total = part if total is None else total + part
    partial_ref[0] = total


def nearness(z, rank):
    low = jnp.minimum(z, 3 - z)
    seen = jnp.where((low == 1) & (rank < 2), 1 - rank, rank)
    return jnp.where(z < 2, seen, 3 - seen)


def mesh_kernel(
    offset_hbm,
    lag_hbm,
    record_ref,
    target_ref,
    base_ref,
    flat_ref,
    own_ref,
    gram_ref,
    gram_in,
    offset_ref,
    lag_ref,
    held,
    wins,
    tiles,
    parts,
    sib_in,
    sib_out,
    yin_a,
    yin_b,
    yout_a,
    yout_b,
    zin_a,
    zin_b,
    zout_a,
    zout_b,
    offset_sem,
    lag_sem,
    record_sem,
    tile_sem,
    win_sib_send,
    win_sib_recv,
    win_az_send,
    win_az_recv,
    win_ay_send,
    win_ay_recv,
    win_by_send,
    win_by_recv,
    win_bz_send,
    win_bz_recv,
    sum_sib_send,
    sum_sib_recv,
    sum_ay_send,
    sum_ay_recv,
    sum_az_send,
    sum_az_recv,
    sum_bz_send,
    sum_bz_recv,
    sum_by_send,
    sum_by_recv,
    gram_send,
    gram_recv,
):
    rows, length = record_ref.shape
    regions = target_ref.shape[2]
    weight = SAMPLES / regions
    group = lax.axis_index("groups")
    region = lax.axis_index("region")
    z = lax.div(region, 4)
    y = lax.rem(lax.div(region, 2), 2)
    k = lax.rem(region, 2)
    other = 1 - y
    sibling = 4 * z + 2 * y + 1 - k
    partner = 4 * z + 2 * other + k
    ahead = (region + 4, region - 4)
    has_next = (z < 3, z > 0)
    has_prev = (z > 0, z < 3)
    sign = (1, -1)
    first = (z, 3 - z)
    part_a = pl.ds(0, PART_A)
    part_b = pl.ds(PART_A, WIDE - PART_A)

    def chip(zz, yy):
        return 2 * zz + yy

    def remote(src, dst, send, recv, device):
        return pltpu.make_async_remote_copy(
            src_ref=src,
            dst_ref=dst,
            send_sem=send,
            recv_sem=recv,
            device_id=(group, device),
            device_id_type=pl.DeviceIdType.MESH,
        )

    def win_sib(p, lane):
        ref = wins.at[p, lane]
        return remote(ref, ref, win_sib_send.at[p], win_sib_recv.at[p], sibling)

    def win_az(way, zs):
        ref = wins.at[chip(zs, y), k, part_a]
        return remote(ref, ref, win_az_send.at[way, zs], win_az_recv.at[zs], ahead[way])

    def win_ay(zs, line):
        ref = wins.at[chip(zs, line), k, part_a]
        return remote(ref, ref, win_ay_send.at[zs], win_ay_recv.at[zs], partner)

    def win_by(line):
        ref = wins.at[chip(z, line), k, part_b]
        return remote(ref, ref, win_by_send, win_by_recv, partner)

    def win_bz(way, line, zs):
        ref = wins.at[chip(zs, line), k, part_b]
        return remote(
            ref, ref, win_bz_send.at[way, line, zs], win_bz_recv.at[line, zs], ahead[way]
        )

    def sum_sib(slot, p):
        return remote(
            sib_out.at[slot], sib_in.at[p], sum_sib_send.at[slot], sum_sib_recv.at[p], sibling
        )

    def sum_ay(zd):
        return remote(yout_a.at[zd], yin_a.at[zd], sum_ay_send.at[zd], sum_ay_recv.at[zd], partner)

    def sum_az(way, zd):
        return remote(
            zout_a.at[zd],
            zin_a.at[way, zd],
            sum_az_send.at[zd],
            sum_az_recv.at[way, zd],
            ahead[way],
        )

    def sum_bz(way, line, zd):
        return remote(
            zout_b.at[line, zd],
            zin_b.at[way, line, zd],
            sum_bz_send.at[line, zd],
            sum_bz_recv.at[way, line, zd],
            ahead[way],
        )

    def sum_by():
        return remote(yout_b, yin_b, sum_by_send, sum_by_recv, partner)

    def send_order(j):
        return nearness(z, 3 - lax.div(j, 2)), jnp.where(lax.rem(j, 2) == 0, other, y)

    def tile_chip(n):
        zd, line = send_order(n)
        m = n - 8
        zs = nearness(z, lax.div(m, 2))
        turn = jnp.where(lax.rem(m, 2) == 0, y, other)
        return jnp.where(n < 8, chip(zd, line), chip(zs, turn))

    def tile_copy(n):
        column = pl.multiple_of(tile_chip(n) * 2 * rows, 2 * rows)
        slot = lax.rem(n, 2)
        return pltpu.make_async_copy(
            target_ref.at[:, :, pl.ds(column, 2 * rows)], tiles.at[slot], tile_sem.at[slot]
        )

    def next_tile(n):
        @pl.when(n < 15)
        def _():
            tile_copy(n + 1).start()

        tile_copy(n).wait()

    fetch = pltpu.make_async_copy(record_ref, held, record_sem)
    fetch_offset = pltpu.make_async_copy(offset_hbm, offset_ref, offset_sem)
    fetch_lag = pltpu.make_async_copy(lag_hbm, lag_ref, lag_sem)
    fetch_offset.start()
    fetch.start()
    fetch_lag.start()
    tile_copy(0).start()
    here = chip(z, y)
    barrier = pltpu.get_barrier_semaphore()
    for device, there in (
        (sibling, None),
        (partner, None),
        (ahead[0], has_next[0]),
        (ahead[1], has_next[1]),
    ):

        def greet(device=device):
            pl.semaphore_signal(
                barrier, inc=1, device_id=(group, device), device_id_type=pl.DeviceIdType.MESH
            )

        if there is None:
            greet()
        else:
            pl.when(there)(greet)
    fetch_offset.wait()
    fetch_lag.wait()
    sample = lax.broadcasted_iota(jnp.int32, (WIDE, length), 0)
    column = lax.broadcasted_iota(jnp.int32, (WIDE, length), 1) - offset_ref[0]
    pick = jnp.where(column == sample, 1.0, 0.0).astype(jnp.bfloat16)
    fetch.wait()

    def cut(first, last):
        wins[here, k, first:last] = lax.dot_general(
            pick[first:last],
            held[...],
            (((1,), (1,)), ((), ())),
            preferred_element_type=jnp.float32,
        ).astype(jnp.bfloat16)

    cut(0, PART_A)
    pl.semaphore_wait(barrier, 2 + (z < 3).astype(jnp.int32) + (z > 0).astype(jnp.int32))
    for way in range(2):

        @pl.when(has_next[way])
        def _():
            win_az(way, z).start()

    cut(PART_A, WIDE)
    win_by(y).start()
    for way in range(2):

        @pl.when(has_next[way])
        def _():
            win_bz(way, y, z).start()

    win_sib(here, k).start()
    window = wins[here, k]

    own_ref[...] = jnp.zeros_like(own_ref)
    gram_ref[...] = jnp.zeros_like(gram_ref)
    flat_ref[:SAMPLES, :rows] = window[:SAMPLES]
    flat_ref[SAMPLES:, :rows] = jnp.zeros((WIDE - SAMPLES, rows), jnp.bfloat16)
    sample = lax.broadcasted_iota(jnp.int32, (WIDE, SAMPLES), 0)
    column = lax.broadcasted_iota(jnp.int32, (WIDE, SAMPLES), 1)
    pick = jnp.concatenate(
        [jnp.where(column + lag_ref[term] == sample, 1.0, 0.0) for term in range(LAGS)]
    ).astype(jnp.bfloat16)
    moved = jnp.dot(pick, window[:SAMPLES], preferred_element_type=jnp.float32)
    for term in range(LAGS):
        flat_ref[:, (1 + term) * rows : (2 + term) * rows] = moved[
            term * WIDE : (term + 1) * WIDE
        ].astype(jnp.bfloat16)

    def collect(j):
        zd, line = send_order(j)
        p = chip(zd, line)
        sum_sib(lax.rem(j, 2), p).wait_recv()
        parts[p] += sib_in[p]

        @pl.when(lax.rem(j, 2) == 0)
        def _():
            yout_a[zd] = parts[p, part_a].astype(jnp.bfloat16)

            @pl.when(j < 6)
            def _():
                sum_ay(zd).start()

    def relay_a(s, way):
        zs = z - sign[way] * s
        zd = z + sign[way] * (4 - s)

        @pl.when(first[way] >= s)
        def _():
            win_az(way, zs).wait_recv()

            @pl.when(has_next[way])
            def _():
                win_az(way, zs).start()

            win_ay(zs, y).start()

        return zd

    def forward_a(s, way):
        zd = z + sign[way] * (4 - s)

        @pl.when(first[way] < s)
        def _():
            sum_ay(zd).wait_recv()
            p = chip(zd, y)

            @pl.when(has_prev[way])
            def _():
                sum_az(way, zd).wait_recv()
                zout_a[zd] = (
                    parts[p, part_a]
                    + yin_a[zd].astype(jnp.float32)
                    + zin_a[way, zd].astype(jnp.float32)
                ).astype(jnp.bfloat16)

            @pl.when(jnp.logical_not(has_prev[way]))
            def _():
                zout_a[zd] = (parts[p, part_a] + yin_a[zd].astype(jnp.float32)).astype(
                    jnp.bfloat16
                )

            sum_az(way, zd).start()

    def relay_b(s, way, line):
        zs = z - sign[way] * s

        @pl.when(first[way] >= s)
        def _():
            win_bz(way, line, zs).wait_recv()

            @pl.when(has_next[way])
            def _():
                win_bz(way, line, zs).start()

    def share(s, way):
        zs = z - sign[way] * s

        @pl.when(first[way] >= s)
        def _():
            win_sib(chip(zs, y), k).start()

    def forward_b(s, way, line):
        zd = z + sign[way] * (4 - s)

        @pl.when(first[way] < s)
        def _():
            p = chip(zd, line)

            @pl.when(has_prev[way])
            def _():
                sum_bz(way, line, zd).wait_recv()
                zout_b[line, zd] = (
                    parts[p, part_b] + zin_b[way, line, zd].astype(jnp.float32)
                ).astype(jnp.bfloat16)

            @pl.when(jnp.logical_not(has_prev[way]))
            def _():
                zout_b[line, zd] = parts[p, part_b].astype(jnp.bfloat16)

            sum_bz(way, line, zd).start()

    def bracket(s, piece):
        for way in range(2):
            if piece == 0:
                relay_a(s, way)
                forward_b(s, way, other)
            elif piece == 1:
                relay_b(s, way, y)
                share(s, way)
                forward_a(s, way)
            else:
                relay_b(s, way, other)
                forward_b(s, way, y)

    def pass_on():
        win_by(other).wait_recv()
        for way in range(2):

            @pl.when(has_next[way])
            def _():
                win_bz(way, other, z).start()

    def finish_across():
        across = chip(z, other)
        for way in range(2):

            @pl.when(has_prev[way])
            def _():
                sum_bz(way, other, z).wait_recv()
                parts[across, part_b] += zin_b[way, other, z].astype(jnp.float32)

        yout_b[...] = parts[across, part_b].astype(jnp.bfloat16)
        sum_by().start()

    def at(step, table):
        for when, actions in table:

            @pl.when(step == when)
            def _():
                for action in actions:
                    action()

    def relay(s, piece):
        return lambda: bracket(s, piece)

    def send_step(j, carry):
        at(
            j,
            (
                (1, (lambda: win_ay(z, y).start(),)),
                (2, (pass_on,)),
                (3, (relay(1, 0),)),
                (5, (relay(1, 1),)),
                (6, (relay(1, 2),)),
                (7, (relay(2, 0),)),
            ),
        )
        next_tile(j)
        slot = lax.rem(j, 2)
        zd, line = send_order(j)
        p = chip(zd, line)

        @pl.when(j > 1)
        def _():
            sum_sib(slot, p).wait_send()

        def product(lane):
            column = pl.multiple_of(lane * rows, rows)
            tile = tiles[slot, :, :, pl.ds(column, rows)].reshape(TERMS * rows, rows)
            return jnp.dot(flat_ref[...], tile, preferred_element_type=jnp.float32)

        sib_out[slot] = product(1 - k)
        sum_sib(slot, p).start()
        parts[p] = product(k)

        @pl.when(j > 0)
        def _():
            collect(j - 1)

        return carry

    lax.fori_loop(0, 8, send_step, 0)
    bracket(2, 1)
    bracket(2, 2)
    collect(7)

    def use(n, p):
        next_tile(n)
        slot = lax.rem(n, 2)
        win_sib(p, 1 - k).wait_recv()
        window = jnp.concatenate([wins[p, 0], wins[p, 1]], axis=1)
        for term in range(TERMS):
            own_ref[term] += lax.dot_general(
                window,
                tiles[slot, term],
                (((1,), (1,)), ((), ())),
                preferred_element_type=jnp.float32,
            )

    def gram_copy():
        return remote(gram_ref, gram_in, gram_send, gram_recv, sibling)

    def open_round(rank):
        zs = nearness(z, rank)
        win_ay(zs, other).wait_recv()
        win_sib(chip(zs, other), k).start()
        pair = jnp.concatenate([wins[chip(zs, y), k], wins[chip(zs, other), k]], axis=1)
        gram_ref[...] += lax.dot_general(
            pair, pair, (((1,), (1,)), ((), ())), preferred_element_type=jnp.float32
        )

        @pl.when(rank == 3)
        def _():
            gram_copy().start()

    def use_step(n, carry):
        at(
            n,
            (
                (3, (relay(3, 0),)),
                (4, (lambda: sum_ay(z).start(),)),
                (5, (relay(3, 1),)),
                (6, (relay(3, 2), finish_across)),
            ),
        )
        rank = lax.div(n, 2)

        @pl.when(lax.rem(n, 2) == 0)
        def _():
            open_round(rank)

        use(8 + n, chip(nearness(z, rank), jnp.where(lax.rem(n, 2) == 0, y, other)))
        return carry

    lax.fori_loop(0, 8, use_step, 0)

    gram_copy().wait_recv()
    gram = jnp.concatenate(
        [gram_ref[...] + gram_in[...], jnp.zeros((WIDE, WIDTH - WIDE), jnp.float32)], axis=1
    )
    inside = (lax.broadcasted_iota(jnp.int32, gram.shape, 0) < SAMPLES) & (
        lax.broadcasted_iota(jnp.int32, gram.shape, 1) < SAMPLES
    )
    early_gram = jnp.where(inside, gram, 0.0)
    before = 2.0 * gram
    after = jnp.zeros_like(gram)
    early = own_ref[0, :SAMPLES]
    for term in range(LAGS):
        lag = lag_ref[term]
        before += pltpu.roll(pltpu.roll(gram, WIDE - lag, 0), WIDTH - lag, 1)
        after += pltpu.roll(pltpu.roll(early_gram, lag, 0), lag, 1)
        moved = own_ref[1 + term, 1:SPAN]
        for step in (4, 2, 1):
            size = moved.shape[0] - step
            moved = jnp.where(((lag - 1) & step) > 0, moved[step:], moved[:size])
        early = early + moved
    mixed = (jnp.where(inside, before, 0.0) + after)[:, :WIDE]
    coarse = mixed.astype(jnp.bfloat16)
    fine = (mixed - coarse.astype(jnp.float32)).astype(jnp.bfloat16)
    window = wins[here, k]
    smooth = jnp.dot(coarse, window, preferred_element_type=jnp.float32) + jnp.dot(
        fine, window, preferred_element_type=jnp.float32
    )
    base_ref[...] = smooth * (1.0 / regions) - weight * parts[here]
    base_ref[:SAMPLES] -= weight * early

    sum_ay(z).wait_recv()
    base_ref[part_a] -= weight * yin_a[z].astype(jnp.float32)
    for way in range(2):

        @pl.when(has_prev[way])
        def _():
            sum_az(way, z).wait_recv()
            base_ref[part_a] -= weight * zin_a[way, z].astype(jnp.float32)

    sum_by().wait_recv()
    base_ref[part_b] -= weight * yin_b[...].astype(jnp.float32)
    for way in range(2):

        @pl.when(has_prev[way])
        def _():
            sum_bz(way, y, z).wait_recv()
            base_ref[part_b] -= weight * zin_b[way, y, z].astype(jnp.float32)

    gram_copy().wait_send()
    win_by(y).wait_send()
    sum_by().wait_send()
    for slot in range(2):
        sum_sib(slot, here).wait_send()

    def drain(i, carry):
        win_ay(i, y).wait_send()
        sum_ay(i).wait_send()
        for line in range(2):
            win_sib(chip(i, line), k).wait_send()
        for way in range(2):
            reached = (i <= z, i >= z)[way]
            beyond = (i > z, i < z)[way]

            @pl.when(reached & has_next[way])
            def _():
                win_az(way, i).wait_send()
                for line in range(2):
                    win_bz(way, line, i).wait_send()

            @pl.when(beyond)
            def _():
                sum_az(way, i).wait_send()
                for line in range(2):
                    sum_bz(way, line, i).wait_send()

        return carry

    lax.fori_loop(0, 4, drain, 0)


def turn_kernel(
    offset_hbm, base_ref, grad_ref, offset_ref, held, result, offset_sem, arrive, leave
):
    slabs, size, length = result.shape
    fetch = pltpu.make_async_copy(offset_hbm, offset_ref, offset_sem)
    fetch.start()
    came, left = [], []
    for slab in range(slabs):
        lines = pl.ds(slab * size, size)
        came.append(pltpu.make_async_copy(base_ref.at[:, lines], held.at[slab], arrive.at[slab]))
        left.append(pltpu.make_async_copy(result.at[slab], grad_ref.at[lines], leave.at[slab]))
        came[slab].start()
    fetch.wait()
    for slab in range(slabs):
        came[slab].wait()
        turned = jnp.concatenate(
            [held[slab].T, jnp.zeros((size, length - WIDE), jnp.float32)], axis=1
        )
        result[slab] = pltpu.roll(turned, offset_ref[0], 1)
        left[slab].start()
    for slab in range(slabs):
        left[slab].wait()


def mesh_shards(record, target, offset, lag_steps):
    rows, length = record.shape
    regions = target.shape[2]
    rest = WIDE - PART_A
    work = 4 * TERMS * rows * regions * WIDE
    dma = pltpu.SemaphoreType.DMA
    half, full = jnp.bfloat16, jnp.float32
    base = pl.pallas_call(
        mesh_kernel,
        in_specs=[pl.BlockSpec(memory_space=pl.ANY)] * 4,
        out_specs=pl.BlockSpec(memory_space=pltpu.VMEM),
        out_shape=jax.ShapeDtypeStruct((WIDE, rows), full),
        scratch_shapes=[
            pltpu.VMEM((WIDE, TERMS * rows), half),
            pltpu.VMEM((TERMS, WIDE, rows), full),
            pltpu.VMEM((WIDE, WIDE), full),
            pltpu.VMEM((WIDE, WIDE), full),
            pltpu.SMEM((1,), jnp.int32),
            pltpu.SMEM((LAGS,), jnp.int32),
            pltpu.VMEM((rows, length), half),
            pltpu.VMEM((8, 2, WIDE, rows), half),
            pltpu.VMEM((2, TERMS, rows, 2 * rows), half),
            pltpu.VMEM((8, WIDE, rows), full),
            pltpu.VMEM((8, WIDE, rows), full),
            pltpu.VMEM((2, WIDE, rows), full),
            pltpu.VMEM((4, PART_A, rows), half),
            pltpu.VMEM((rest, rows), half),
            pltpu.VMEM((4, PART_A, rows), half),
            pltpu.VMEM((rest, rows), half),
            pltpu.VMEM((2, 4, PART_A, rows), half),
            pltpu.VMEM((2, 2, 4, rest, rows), half),
            pltpu.VMEM((4, PART_A, rows), half),
            pltpu.VMEM((2, 4, rest, rows), half),
            dma,
            dma,
            dma,
            dma((2,)),
            dma((8,)),
            dma((8,)),
            dma((2, 4)),
            dma((4,)),
            dma((4,)),
            dma((4,)),
            dma,
            dma,
            dma((2, 2, 4)),
            dma((2, 4)),
            dma((2,)),
            dma((8,)),
            dma((4,)),
            dma((4,)),
            dma((4,)),
            dma((2, 4)),
            dma((2, 4)),
            dma((2, 2, 4)),
            dma,
            dma,
            dma,
            dma,
        ],
        compiler_params=pltpu.CompilerParams(
            collective_id=0, has_side_effects=True, vmem_limit_bytes=60 << 20
        ),
        cost_estimate=pl.CostEstimate(flops=work, bytes_accessed=70 << 20, transcendentals=0),
        name="mesh",
    )(offset, lag_steps, record, target)
    slabs = rows // SLAB
    return pl.pallas_call(
        turn_kernel,
        in_specs=[pl.BlockSpec(memory_space=pl.ANY)] * 2,
        out_specs=pl.BlockSpec(memory_space=pl.ANY),
        out_shape=jax.ShapeDtypeStruct((rows, length), full),
        scratch_shapes=[
            pltpu.SMEM((1,), jnp.int32),
            pltpu.VMEM((slabs, WIDE, SLAB), full),
            pltpu.VMEM((slabs, SLAB, length), full),
            dma,
            dma((slabs,)),
            dma((slabs,)),
        ],
        name="turn",
    )(offset, base)


def gather_call(regions, devices, scaled, flat, turned, target):
    rows = target.shape[1]
    gathered = lax.all_gather(turned, "region")
    blocks = regions // WIDTH
    if rows != WIDTH:
        gathered = (
            gathered.reshape(blocks, WIDTH // rows, WIDE, rows)
            .transpose(0, 2, 1, 3)
            .reshape(blocks, WIDE, WIDTH)
        )
    partials, own = pl.pallas_call(
        lambda *refs: block_kernel(SAMPLES / regions, *refs),
        grid=(blocks,),
        in_specs=[
            pl.BlockSpec((TERMS, rows, WIDE), lambda i: (0, 0, 0)),
            pl.BlockSpec((SPAN, TERMS * rows), lambda i: (0, 0)),
            pl.BlockSpec((1, WIDE, WIDTH), lambda i: (i, 0, 0)),
            pl.BlockSpec((TERMS, rows, WIDTH), lambda i: (0, 0, i)),
        ],
        out_specs=[
            pl.BlockSpec((1, SPAN, WIDTH), lambda i: (i, 0, 0)),
            pl.BlockSpec((TERMS, WIDE, rows), lambda i: (0, 0, 0)),
        ],
        out_shape=[
            jax.ShapeDtypeStruct((blocks, SPAN, WIDTH), jnp.float32),
            jax.ShapeDtypeStruct((TERMS, WIDE, rows), jnp.float32),
        ],
        compiler_params=pltpu.CompilerParams(vmem_limit_bytes=56 << 20),
        name="blocks",
    )(scaled, flat, gathered, target)
    if rows != WIDTH:
        partials = (
            partials.reshape(blocks, SPAN, WIDTH // rows, rows)
            .transpose(0, 2, 1, 3)
            .reshape(devices, SPAN, rows)
        )
    summed = lax.psum_scatter(partials, "region", scatter_dimension=0, tiled=True)[0]
    return summed, own


def shards(record, target, offset, lag_steps):
    rows = record.shape[0]
    regions = target.shape[2]
    devices = lax.axis_size("region")
    if rows == WIDTH and devices == 16:
        return mesh_shards(record, target, offset, lag_steps)
    begin_at = offset[0]
    window = lax.dynamic_slice_in_dim(record, begin_at, WIDE, 1)
    stacked, shifts = placed_early(window[:, :SAMPLES], lag_steps)
    scaled = stacked * jnp.bfloat16(1.0 / regions)
    flat = stacked[:, :, :SPAN].transpose(2, 0, 1).reshape(SPAN, TERMS * rows)
    turned = window.T
    summed, own = gather_call(regions, devices, scaled, flat, turned, target)
    early = None
    for term in range(TERMS):
        part = lax.dynamic_slice(own[term], (shifts[term], 0), (SAMPLES, rows))
        early = part if early is None else early + part
    in_window = summed + jnp.pad(early, ((0, MAXLAG), (0, 0)))
    grad = jnp.zeros((record.shape[1], rows), jnp.float32)
    return lax.dynamic_update_slice(grad, in_window, (begin_at, 0)).T


def solution(mesh):
    placed = (
        P(("groups", "region"), None),
        P(None, ("groups", "region"), None),
        P("groups"),
        P("groups"),
    )
    return jax.shard_map(
        shards, mesh=mesh, in_specs=placed, out_specs=P(("groups", "region"), None), check_vma=False
    )
```

```python
import jax
import jax.numpy as jnp
from jax import lax
from jax.experimental import pallas as pl
from jax.experimental.pallas import tpu as pltpu
from jax.sharding import PartitionSpec as P

SAMPLES = 384
MAXLAG = 8
LAGS = 3
TERMS = 1 + LAGS
WIDE = 400
SPAN = SAMPLES + MAXLAG
WIDTH = 512
PART_A = 240
SLAB = 128


def placed_early(early, lag_steps):
    rows = early.shape[0]
    shifts = jnp.concatenate([jnp.zeros((1,), jnp.int32), lag_steps])
    padded = jnp.pad(early, ((0, 0), (MAXLAG, WIDE - SAMPLES)))
    parts = [
        lax.dynamic_slice(padded, (0, MAXLAG - shifts[term]), (rows, WIDE)) for term in range(TERMS)
    ]
    return jnp.stack(parts), shifts


def block_kernel(weight, scaled_ref, flat_ref, window_ref, target_ref, partial_ref, own_ref):
    rows = target_ref.shape[1]

    @pl.when(pl.program_id(0) == 0)
    def _():
        own_ref[...] = jnp.zeros_like(own_ref)

    window = window_ref[0]
    total = None
    for term in range(TERMS):
        cov = jnp.dot(scaled_ref[term], window, preferred_element_type=jnp.float32)
        error = (cov - weight * target_ref[term].astype(jnp.float32)).astype(jnp.bfloat16)
        own_ref[term] += lax.dot_general(
            window, error, (((1,), (1,)), ((), ())), preferred_element_type=jnp.float32
        )
        part = jnp.dot(
            flat_ref[:, term * rows : (term + 1) * rows], error, preferred_element_type=jnp.float32
        )
        total = part if total is None else total + part
    partial_ref[0] = total


def nearness(z, rank):
    low = jnp.minimum(z, 3 - z)
    seen = jnp.where((low == 1) & (rank < 2), 1 - rank, rank)
    return jnp.where(z < 2, seen, 3 - seen)


def mesh_kernel(
    offset_hbm,
    lag_hbm,
    record_ref,
    target_ref,
    base_ref,
    flat_ref,
    own_ref,
    gram_ref,
    gram_in,
    offset_ref,
    lag_ref,
    held,
    wins,
    tiles,
    parts,
    sib_in,
    sib_out,
    yin_a,
    yin_b,
    yout_a,
    yout_b,
    zin_a,
    zin_b,
    zout_a,
    zout_b,
    offset_sem,
    lag_sem,
    record_sem,
    tile_sem,
    win_sib_send,
    win_sib_recv,
    win_az_send,
    win_az_recv,
    win_ay_send,
    win_ay_recv,
    win_by_send,
    win_by_recv,
    win_bz_send,
    win_bz_recv,
    sum_sib_send,
    sum_sib_recv,
    sum_ay_send,
    sum_ay_recv,
    sum_az_send,
    sum_az_recv,
    sum_bz_send,
    sum_bz_recv,
    sum_by_send,
    sum_by_recv,
    gram_send,
    gram_recv,
):
    rows, length = record_ref.shape
    regions = target_ref.shape[2]
    weight = SAMPLES / regions
    group = lax.axis_index("groups")
    region = lax.axis_index("region")
    z = lax.div(region, 4)
    y = lax.rem(lax.div(region, 2), 2)
    k = lax.rem(region, 2)
    other = 1 - y
    sibling = 4 * z + 2 * y + 1 - k
    partner = 4 * z + 2 * other + k
    ahead = (region + 4, region - 4)
    has_next = (z < 3, z > 0)
    has_prev = (z > 0, z < 3)
    sign = (1, -1)
    first = (z, 3 - z)
    part_a = pl.ds(0, PART_A)
    part_b = pl.ds(PART_A, WIDE - PART_A)

    def chip(zz, yy):
        return 2 * zz + yy

    def remote(src, dst, send, recv, device):
        return pltpu.make_async_remote_copy(
            src_ref=src,
            dst_ref=dst,
            send_sem=send,
            recv_sem=recv,
            device_id=(group, device),
            device_id_type=pl.DeviceIdType.MESH,
        )

    def win_sib(p, lane):
        ref = wins.at[p, lane]
        return remote(ref, ref, win_sib_send.at[p], win_sib_recv.at[p], sibling)

    def win_az(way, zs):
        ref = wins.at[chip(zs, y), k, part_a]
        return remote(ref, ref, win_az_send.at[way, zs], win_az_recv.at[zs], ahead[way])

    def win_ay(zs, line):
        ref = wins.at[chip(zs, line), k, part_a]
        return remote(ref, ref, win_ay_send.at[zs], win_ay_recv.at[zs], partner)

    def win_by(line):
        ref = wins.at[chip(z, line), k, part_b]
        return remote(ref, ref, win_by_send, win_by_recv, partner)

    def win_bz(way, line, zs):
        ref = wins.at[chip(zs, line), k, part_b]
        return remote(
            ref, ref, win_bz_send.at[way, line, zs], win_bz_recv.at[line, zs], ahead[way]
        )

    def sum_sib(slot, p):
        return remote(
            sib_out.at[slot], sib_in.at[p], sum_sib_send.at[slot], sum_sib_recv.at[p], sibling
        )

    def sum_ay(zd):
        return remote(yout_a.at[zd], yin_a.at[zd], sum_ay_send.at[zd], sum_ay_recv.at[zd], partner)

    def sum_az(way, zd):
        return remote(
            zout_a.at[zd],
            zin_a.at[way, zd],
            sum_az_send.at[zd],
            sum_az_recv.at[way, zd],
            ahead[way],
        )

    def sum_bz(way, line, zd):
        return remote(
            zout_b.at[line, zd],
            zin_b.at[way, line, zd],
            sum_bz_send.at[line, zd],
            sum_bz_recv.at[way, line, zd],
            ahead[way],
        )

    def sum_by():
        return remote(yout_b, yin_b, sum_by_send, sum_by_recv, partner)

    def send_order(j):
        return nearness(z, 3 - lax.div(j, 2)), jnp.where(lax.rem(j, 2) == 0, other, y)

    def tile_chip(n):
        zd, line = send_order(n)
        m = n - 8
        zs = nearness(z, lax.div(m, 2))
        turn = jnp.where(lax.rem(m, 2) == 0, y, other)
        return jnp.where(n < 8, chip(zd, line), chip(zs, turn))

    def tile_copy(n):
        column = pl.multiple_of(tile_chip(n) * 2 * rows, 2 * rows)
        slot = lax.rem(n, 2)
        return pltpu.make_async_copy(
            target_ref.at[:, :, pl.ds(column, 2 * rows)], tiles.at[slot], tile_sem.at[slot]
        )

    def next_tile(n):
        @pl.when(n < 15)
        def _():
            tile_copy(n + 1).start()

        tile_copy(n).wait()

    fetch = pltpu.make_async_copy(record_ref, held, record_sem)
    fetch_offset = pltpu.make_async_copy(offset_hbm, offset_ref, offset_sem)
    fetch_lag = pltpu.make_async_copy(lag_hbm, lag_ref, lag_sem)
    fetch_offset.start()
    fetch.start()
    fetch_lag.start()
    tile_copy(0).start()
    here = chip(z, y)
    barrier = pltpu.get_barrier_semaphore()
    for device, there in (
        (sibling, None),
        (partner, None),
        (ahead[0], has_next[0]),
        (ahead[1], has_next[1]),
    ):

        def greet(device=device):
            pl.semaphore_signal(
                barrier, inc=1, device_id=(group, device), device_id_type=pl.DeviceIdType.MESH
            )

        if there is None:
            greet()
        else:
            pl.when(there)(greet)
    fetch_offset.wait()
    fetch_lag.wait()
    sample = lax.broadcasted_iota(jnp.int32, (WIDE, length), 0)
    column = lax.broadcasted_iota(jnp.int32, (WIDE, length), 1) - offset_ref[0]
    pick = jnp.where(column == sample, 1.0, 0.0).astype(jnp.bfloat16)
    fetch.wait()

    def cut(first, last):
        wins[here, k, first:last] = lax.dot_general(
            pick[first:last],
            held[...],
            (((1,), (1,)), ((), ())),
            preferred_element_type=jnp.float32,
        ).astype(jnp.bfloat16)

    cut(PART_A, WIDE)
    pl.semaphore_wait(barrier, 2 + (z < 3).astype(jnp.int32) + (z > 0).astype(jnp.int32))
    win_by(y).start()
    for way in range(2):

        @pl.when(has_next[way])
        def _():
            win_bz(way, y, z).start()

    cut(0, PART_A)
    for way in range(2):

        @pl.when(has_next[way])
        def _():
            win_az(way, z).start()

    win_sib(here, k).start()
    window = wins[here, k]

    own_ref[...] = jnp.zeros_like(own_ref)
    gram_ref[...] = jnp.zeros_like(gram_ref)
    flat_ref[:SAMPLES, :rows] = window[:SAMPLES]
    flat_ref[SAMPLES:, :rows] = jnp.zeros((WIDE - SAMPLES, rows), jnp.bfloat16)
    sample = lax.broadcasted_iota(jnp.int32, (WIDE, SAMPLES), 0)
    column = lax.broadcasted_iota(jnp.int32, (WIDE, SAMPLES), 1)
    pick = jnp.concatenate(
        [jnp.where(column + lag_ref[term] == sample, 1.0, 0.0) for term in range(LAGS)]
    ).astype(jnp.bfloat16)
    moved = jnp.dot(pick, window[:SAMPLES], preferred_element_type=jnp.float32)
    for term in range(LAGS):
        flat_ref[:, (1 + term) * rows : (2 + term) * rows] = moved[
            term * WIDE : (term + 1) * WIDE
        ].astype(jnp.bfloat16)

    def collect(j):
        zd, line = send_order(j)
        p = chip(zd, line)
        sum_sib(lax.rem(j, 2), p).wait_recv()
        parts[p] += sib_in[p]

        @pl.when(lax.rem(j, 2) == 0)
        def _():
            yout_a[zd] = parts[p, part_a].astype(jnp.bfloat16)

            @pl.when(j < 6)
            def _():
                sum_ay(zd).start()

    def relay_a(s, way):
        zs = z - sign[way] * s
        zd = z + sign[way] * (4 - s)

        @pl.when(first[way] >= s)
        def _():
            win_az(way, zs).wait_recv()

            @pl.when(has_next[way])
            def _():
                win_az(way, zs).start()

            win_ay(zs, y).start()

        return zd

    def forward_a(s, way):
        zd = z + sign[way] * (4 - s)

        @pl.when(first[way] < s)
        def _():
            sum_ay(zd).wait_recv()
            p = chip(zd, y)

            @pl.when(has_prev[way])
            def _():
                sum_az(way, zd).wait_recv()
                zout_a[zd] = (
                    parts[p, part_a]
                    + yin_a[zd].astype(jnp.float32)
                    + zin_a[way, zd].astype(jnp.float32)
                ).astype(jnp.bfloat16)

            @pl.when(jnp.logical_not(has_prev[way]))
            def _():
                zout_a[zd] = (parts[p, part_a] + yin_a[zd].astype(jnp.float32)).astype(
                    jnp.bfloat16
                )

            sum_az(way, zd).start()

    def relay_b(s, way, line):
        zs = z - sign[way] * s

        @pl.when(first[way] >= s)
        def _():
            win_bz(way, line, zs).wait_recv()

            @pl.when(has_next[way])
            def _():
                win_bz(way, line, zs).start()

    def share(s, way):
        zs = z - sign[way] * s

        @pl.when(first[way] >= s)
        def _():
            win_sib(chip(zs, y), k).start()

    def forward_b(s, way, line):
        zd = z + sign[way] * (4 - s)

        @pl.when(first[way] < s)
        def _():
            p = chip(zd, line)

            @pl.when(has_prev[way])
            def _():
                sum_bz(way, line, zd).wait_recv()
                zout_b[line, zd] = (
                    parts[p, part_b] + zin_b[way, line, zd].astype(jnp.float32)
                ).astype(jnp.bfloat16)

            @pl.when(jnp.logical_not(has_prev[way]))
            def _():
                zout_b[line, zd] = parts[p, part_b].astype(jnp.bfloat16)

            sum_bz(way, line, zd).start()

    def bracket(s, piece):
        for way in range(2):
            if piece == 0:
                relay_a(s, way)
                forward_b(s, way, other)
            elif piece == 1:
                relay_b(s, way, y)
                share(s, way)
                forward_a(s, way)
            else:
                relay_b(s, way, other)
                forward_b(s, way, y)

    def pass_on():
        win_by(other).wait_recv()
        for way in range(2):

            @pl.when(has_next[way])
            def _():
                win_bz(way, other, z).start()

    def finish_across():
        across = chip(z, other)
        for way in range(2):

            @pl.when(has_prev[way])
            def _():
                sum_bz(way, other, z).wait_recv()
                parts[across, part_b] += zin_b[way, other, z].astype(jnp.float32)

        yout_b[...] = parts[across, part_b].astype(jnp.bfloat16)
        sum_by().start()

    def at(step, table):
        for when, actions in table:

            @pl.when(step == when)
            def _():
                for action in actions:
                    action()

    def relay(s, piece):
        return lambda: bracket(s, piece)

    def send_step(j, carry):
        at(
            j,
            (
                (1, (lambda: win_ay(z, y).start(),)),
                (2, (pass_on,)),
                (3, (relay(1, 0),)),
                (5, (relay(1, 1),)),
                (6, (relay(1, 2),)),
                (7, (relay(2, 0),)),
            ),
        )
        next_tile(j)
        slot = lax.rem(j, 2)
        zd, line = send_order(j)
        p = chip(zd, line)

        @pl.when(j > 1)
        def _():
            sum_sib(slot, p).wait_send()

        def product(lane):
            column = pl.multiple_of(lane * rows, rows)
            tile = tiles[slot, :, :, pl.ds(column, rows)].reshape(TERMS * rows, rows)
            return jnp.dot(flat_ref[...], tile, preferred_element_type=jnp.float32)

        sib_out[slot] = product(1 - k)
        sum_sib(slot, p).start()
        parts[p] = product(k)

        @pl.when(j > 0)
        def _():
            collect(j - 1)

        return carry

    lax.fori_loop(0, 8, send_step, 0)
    bracket(2, 1)
    bracket(2, 2)
    collect(7)

    def use(n, p):
        next_tile(n)
        slot = lax.rem(n, 2)
        win_sib(p, 1 - k).wait_recv()
        window = jnp.concatenate([wins[p, 0], wins[p, 1]], axis=1)
        for term in range(TERMS):
            own_ref[term] += lax.dot_general(
                window,
                tiles[slot, term],
                (((1,), (1,)), ((), ())),
                preferred_element_type=jnp.float32,
            )

    def gram_copy():
        return remote(gram_ref, gram_in, gram_send, gram_recv, sibling)

    def open_round(rank):
        zs = nearness(z, rank)
        win_ay(zs, other).wait_recv()
        win_sib(chip(zs, other), k).start()
        pair = jnp.concatenate([wins[chip(zs, y), k], wins[chip(zs, other), k]], axis=1)
        gram_ref[...] += lax.dot_general(
            pair, pair, (((1,), (1,)), ((), ())), preferred_element_type=jnp.float32
        )

        @pl.when(rank == 3)
        def _():
            gram_copy().start()

    def use_step(n, carry):
        at(
            n,
            (
                (3, (relay(3, 0),)),
                (4, (lambda: sum_ay(z).start(),)),
                (5, (relay(3, 1),)),
                (6, (relay(3, 2), finish_across)),
            ),
        )
        rank = lax.div(n, 2)

        @pl.when(lax.rem(n, 2) == 0)
        def _():
            open_round(rank)

        use(8 + n, chip(nearness(z, rank), jnp.where(lax.rem(n, 2) == 0, y, other)))
        return carry

    lax.fori_loop(0, 8, use_step, 0)

    gram_copy().wait_recv()
    gram = jnp.concatenate(
        [gram_ref[...] + gram_in[...], jnp.zeros((WIDE, WIDTH - WIDE), jnp.float32)], axis=1
    )
    inside = (lax.broadcasted_iota(jnp.int32, gram.shape, 0) < SAMPLES) & (
        lax.broadcasted_iota(jnp.int32, gram.shape, 1) < SAMPLES
    )
    early_gram = jnp.where(inside, gram, 0.0)
    before = 2.0 * gram
    after = jnp.zeros_like(gram)
    early = own_ref[0, :SAMPLES]
    for term in range(LAGS):
        lag = lag_ref[term]
        before += pltpu.roll(pltpu.roll(gram, WIDE - lag, 0), WIDTH - lag, 1)
        after += pltpu.roll(pltpu.roll(early_gram, lag, 0), lag, 1)
        moved = own_ref[1 + term, 1:SPAN]
        for step in (4, 2, 1):
            size = moved.shape[0] - step
            moved = jnp.where(((lag - 1) & step) > 0, moved[step:], moved[:size])
        early = early + moved
    mixed = (jnp.where(inside, before, 0.0) + after)[:, :WIDE]
    coarse = mixed.astype(jnp.bfloat16)
    fine = (mixed - coarse.astype(jnp.float32)).astype(jnp.bfloat16)
    window = wins[here, k]
    smooth = jnp.dot(coarse, window, preferred_element_type=jnp.float32) + jnp.dot(
        fine, window, preferred_element_type=jnp.float32
    )
    base_ref[...] = smooth * (1.0 / regions) - weight * parts[here]
    base_ref[:SAMPLES] -= weight * early

    sum_ay(z).wait_recv()
    base_ref[part_a] -= weight * yin_a[z].astype(jnp.float32)
    for way in range(2):

        @pl.when(has_prev[way])
        def _():
            sum_az(way, z).wait_recv()
            base_ref[part_a] -= weight * zin_a[way, z].astype(jnp.float32)

    sum_by().wait_recv()
    base_ref[part_b] -= weight * yin_b[...].astype(jnp.float32)
    for way in range(2):

        @pl.when(has_prev[way])
        def _():
            sum_bz(way, y, z).wait_recv()
            base_ref[part_b] -= weight * zin_b[way, y, z].astype(jnp.float32)

    gram_copy().wait_send()
    win_by(y).wait_send()
    sum_by().wait_send()
    for slot in range(2):
        sum_sib(slot, here).wait_send()

    def drain(i, carry):
        win_ay(i, y).wait_send()
        sum_ay(i).wait_send()
        for line in range(2):
            win_sib(chip(i, line), k).wait_send()
        for way in range(2):
            reached = (i <= z, i >= z)[way]
            beyond = (i > z, i < z)[way]

            @pl.when(reached & has_next[way])
            def _():
                win_az(way, i).wait_send()
                for line in range(2):
                    win_bz(way, line, i).wait_send()

            @pl.when(beyond)
            def _():
                sum_az(way, i).wait_send()
                for line in range(2):
                    sum_bz(way, line, i).wait_send()

        return carry

    lax.fori_loop(0, 4, drain, 0)


def turn_kernel(
    offset_hbm, base_ref, grad_ref, offset_ref, held, result, offset_sem, arrive, leave
):
    slabs, size, length = result.shape
    fetch = pltpu.make_async_copy(offset_hbm, offset_ref, offset_sem)
    fetch.start()
    came, left = [], []
    for slab in range(slabs):
        lines = pl.ds(slab * size, size)
        came.append(pltpu.make_async_copy(base_ref.at[:, lines], held.at[slab], arrive.at[slab]))
        left.append(pltpu.make_async_copy(result.at[slab], grad_ref.at[lines], leave.at[slab]))
        came[slab].start()
    fetch.wait()
    for slab in range(slabs):
        came[slab].wait()
        turned = jnp.concatenate(
            [held[slab].T, jnp.zeros((size, length - WIDE), jnp.float32)], axis=1
        )
        result[slab] = pltpu.roll(turned, offset_ref[0], 1)
        left[slab].start()
    for slab in range(slabs):
        left[slab].wait()


def mesh_shards(record, target, offset, lag_steps):
    rows, length = record.shape
    regions = target.shape[2]
    rest = WIDE - PART_A
    work = 4 * TERMS * rows * regions * WIDE
    dma = pltpu.SemaphoreType.DMA
    half, full = jnp.bfloat16, jnp.float32
    base = pl.pallas_call(
        mesh_kernel,
        in_specs=[pl.BlockSpec(memory_space=pl.ANY)] * 4,
        out_specs=pl.BlockSpec(memory_space=pltpu.VMEM),
        out_shape=jax.ShapeDtypeStruct((WIDE, rows), full),
        scratch_shapes=[
            pltpu.VMEM((WIDE, TERMS * rows), half),
            pltpu.VMEM((TERMS, WIDE, rows), full),
            pltpu.VMEM((WIDE, WIDE), full),
            pltpu.VMEM((WIDE, WIDE), full),
            pltpu.SMEM((1,), jnp.int32),
            pltpu.SMEM((LAGS,), jnp.int32),
            pltpu.VMEM((rows, length), half),
            pltpu.VMEM((8, 2, WIDE, rows), half),
            pltpu.VMEM((2, TERMS, rows, 2 * rows), half),
            pltpu.VMEM((8, WIDE, rows), full),
            pltpu.VMEM((8, WIDE, rows), full),
            pltpu.VMEM((2, WIDE, rows), full),
            pltpu.VMEM((4, PART_A, rows), half),
            pltpu.VMEM((rest, rows), half),
            pltpu.VMEM((4, PART_A, rows), half),
            pltpu.VMEM((rest, rows), half),
            pltpu.VMEM((2, 4, PART_A, rows), half),
            pltpu.VMEM((2, 2, 4, rest, rows), half),
            pltpu.VMEM((4, PART_A, rows), half),
            pltpu.VMEM((2, 4, rest, rows), half),
            dma,
            dma,
            dma,
            dma((2,)),
            dma((8,)),
            dma((8,)),
            dma((2, 4)),
            dma((4,)),
            dma((4,)),
            dma((4,)),
            dma,
            dma,
            dma((2, 2, 4)),
            dma((2, 4)),
            dma((2,)),
            dma((8,)),
            dma((4,)),
            dma((4,)),
            dma((4,)),
            dma((2, 4)),
            dma((2, 4)),
            dma((2, 2, 4)),
            dma,
            dma,
            dma,
            dma,
        ],
        compiler_params=pltpu.CompilerParams(
            collective_id=0, has_side_effects=True, vmem_limit_bytes=60 << 20
        ),
        cost_estimate=pl.CostEstimate(flops=work, bytes_accessed=70 << 20, transcendentals=0),
        name="mesh",
    )(offset, lag_steps, record, target)
    slabs = rows // SLAB
    return pl.pallas_call(
        turn_kernel,
        in_specs=[pl.BlockSpec(memory_space=pl.ANY)] * 2,
        out_specs=pl.BlockSpec(memory_space=pl.ANY),
        out_shape=jax.ShapeDtypeStruct((rows, length), full),
        scratch_shapes=[
            pltpu.SMEM((1,), jnp.int32),
            pltpu.VMEM((slabs, WIDE, SLAB), full),
            pltpu.VMEM((slabs, SLAB, length), full),
            dma,
            dma((slabs,)),
            dma((slabs,)),
        ],
        name="turn",
    )(offset, base)


def gather_call(regions, devices, scaled, flat, turned, target):
    rows = target.shape[1]
    gathered = lax.all_gather(turned, "region")
    blocks = regions // WIDTH
    if rows != WIDTH:
        gathered = (
            gathered.reshape(blocks, WIDTH // rows, WIDE, rows)
            .transpose(0, 2, 1, 3)
            .reshape(blocks, WIDE, WIDTH)
        )
    partials, own = pl.pallas_call(
        lambda *refs: block_kernel(SAMPLES / regions, *refs),
        grid=(blocks,),
        in_specs=[
            pl.BlockSpec((TERMS, rows, WIDE), lambda i: (0, 0, 0)),
            pl.BlockSpec((SPAN, TERMS * rows), lambda i: (0, 0)),
            pl.BlockSpec((1, WIDE, WIDTH), lambda i: (i, 0, 0)),
            pl.BlockSpec((TERMS, rows, WIDTH), lambda i: (0, 0, i)),
        ],
        out_specs=[
            pl.BlockSpec((1, SPAN, WIDTH), lambda i: (i, 0, 0)),
            pl.BlockSpec((TERMS, WIDE, rows), lambda i: (0, 0, 0)),
        ],
        out_shape=[
            jax.ShapeDtypeStruct((blocks, SPAN, WIDTH), jnp.float32),
            jax.ShapeDtypeStruct((TERMS, WIDE, rows), jnp.float32),
        ],
        compiler_params=pltpu.CompilerParams(vmem_limit_bytes=56 << 20),
        name="blocks",
    )(scaled, flat, gathered, target)
    if rows != WIDTH:
        partials = (
            partials.reshape(blocks, SPAN, WIDTH // rows, rows)
            .transpose(0, 2, 1, 3)
            .reshape(devices, SPAN, rows)
        )
    summed = lax.psum_scatter(partials, "region", scatter_dimension=0, tiled=True)[0]
    return summed, own


def shards(record, target, offset, lag_steps):
    rows = record.shape[0]
    regions = target.shape[2]
    devices = lax.axis_size("region")
    if rows == WIDTH and devices == 16:
        return mesh_shards(record, target, offset, lag_steps)
    begin_at = offset[0]
    window = lax.dynamic_slice_in_dim(record, begin_at, WIDE, 1)
    stacked, shifts = placed_early(window[:, :SAMPLES], lag_steps)
    scaled = stacked * jnp.bfloat16(1.0 / regions)
    flat = stacked[:, :, :SPAN].transpose(2, 0, 1).reshape(SPAN, TERMS * rows)
    turned = window.T
    summed, own = gather_call(regions, devices, scaled, flat, turned, target)
    early = None
    for term in range(TERMS):
        part = lax.dynamic_slice(own[term], (shifts[term], 0), (SAMPLES, rows))
        early = part if early is None else early + part
    in_window = summed + jnp.pad(early, ((0, MAXLAG), (0, 0)))
    grad = jnp.zeros((record.shape[1], rows), jnp.float32)
    return lax.dynamic_update_slice(grad, in_window, (begin_at, 0)).T


def solution(mesh):
    placed = (
        P(("groups", "region"), None),
        P(None, ("groups", "region"), None),
        P("groups"),
        P("groups"),
    )
    return jax.shard_map(
        shards, mesh=mesh, in_specs=placed, out_specs=P(("groups", "region"), None), check_vma=False
    )
```
